32 devices in a mesh: groups: 2 (over x), views: 16 (over z, y, core).
Axes of the slice: x: 2, y: 2, z: 4, core: 2. Of those that a mesh axis runs over, the one named last changes fastest.
Arguments:
- tokens: bfloat16 [32, 128, 1024], P(('groups', 'views')), parts along dimension 0, may hold values from -6 to 6
- in_gain: float32 [1024], replicated, may hold values from 0.7 to 6, as said below
- w_query: bfloat16 [1024, 1024], replicated, may hold values from -0.1875 to 0.1875
- w_key: bfloat16 [1024, 1024], replicated, may hold values from -0.1875 to 0.1875
- w_value: bfloat16 [1024, 1024], replicated, may hold values from -0.1875 to 0.1875
- w_out: bfloat16 [1024, 1024], replicated, may hold values from -0.1875 to 0.1875
- out_gain: float32 [1024], replicated, may hold values from 0.1 to 1.9
- covis_list: int32 [32, 12], P(('groups', 'views')), parts along dimension 0, may hold values from 0 to 15, as said below
- covis_count: int32 [32], P(('groups', 'views')), parts along dimension 0, may hold values from 2 to 12
Outputs:
- mixed: bfloat16 [32, 128, 1024], P(('groups', 'views')), parts along dimension 0
The draws below stay inside these ranges and needn't reach their ends.
There are 2 independent parts, one for each index of `groups`. The reference program is written for one: setup_inputs(seed, part) draws one part's arguments, and reference() takes and returns one part's arrays. A program takes and returns all parts, laid end to end along the dimension named above; an argument that names none is the same for every part. Nothing has to cross between parts.
Inputs may be any that keep to these rules, and one draw needn't show every extreme that they name: `covis_list`: row v lists 12 distinct view ids w, each with w - v modulo 16 among -6 to -1 and 1 to 6; only the first covis_count[v] entries are covisible views, the others are not used. `in_gain`: positive gains.
All inputs are finite; a program needn't handle non-finite values.
Results may differ from the reference program's by a relative error of at most 0.0085.
The reference program's roundings to bfloat16 on the way (of `normed`, `weights` and `head_normed`) count: a program that leaves them out, or rounds other values in their place, can miss the bound.
Values may be sent and summed in bfloat16 or wider, within the bound.
A program may use at most 128 MiB of HBM per device.

```python
import jax
import jax.numpy as jnp
from jax import lax

D = 1024
HEADS = 16
HEAD_DIM = 64
TOK_VIEW = 128
REACH = 6
MAXCOV = 12
VIEWS = 16


def draw_in_gain(key, part):
    return jax.random.uniform(key, (D,), jnp.float32, 0.7, 1.3)


def covis_tables(key):
    base = jax.random.fold_in(key, 11)
    key_first, key_second, key_pick, key_other, key_order = jax.random.split(base, 5)
    span = 2 * REACH
    first = jax.random.randint(key_first, (VIEWS,), 0, span - 1)
    second = jax.random.randint(key_second, (VIEWS,), 0, span - 1)
    counts = 2 + first * second // (span - 2)
    pick = jax.random.randint(key_pick, (), 0, VIEWS)
    other = (pick + 1 + jax.random.randint(key_other, (), 0, VIEWS - 1)) % VIEWS
    counts = counts.at[pick].set(span).at[other].set(2)
    slot = jnp.arange(span, dtype=jnp.int32)
    offsets = jnp.where(slot < REACH, slot - REACH, slot - REACH + 1)
    ranking = jax.random.randint(key_order, (VIEWS, span), 0, 1 << 20) * span + slot[None, :]
    order = jnp.argsort(ranking, axis=1)
    chosen = offsets[order]
    ids = (jnp.arange(VIEWS, dtype=jnp.int32)[:, None] + chosen) % VIEWS
    return (ids.astype(jnp.int32), counts.astype(jnp.int32))


def draw_covis_list(key, part):
    return covis_tables(key)[0]


def draw_covis_count(key, part):
    return covis_tables(key)[1]


def level_of(rng, shape, shards, smallest, top_value):
    def one(position, parts):
        steps = jax.random.uniform(jax.random.fold_in(jax.random.fold_in(rng, 6), position), (parts,), jnp.float32, smallest / len(shards), top_value / len(shards))
        return jnp.repeat(jnp.exp(steps), shape[position] // parts).reshape((-1,) + (1,) * (len(shape) - position - 1))

    factor_of = one(*shards[0])
    for cut in shards[1:]:
        factor_of = factor_of * one(*cut)
    return factor_of


def gaussian(stream_key, extent, width, limit, cuts=(), held_as=jnp.bfloat16):
    loudness = level_of(stream_key, extent, cuts, -0.22, 0.18) if cuts else 1.0
    values = jax.random.normal(stream_key, extent, jnp.float32) * width * loudness
    return jnp.minimum(jnp.maximum(values, -limit), limit).astype(held_as)


def setup_inputs(seed: int = 0, part: int = 0) -> dict:
    arg_keys = jax.random.split(jax.random.key(seed), 10)
    part_keys = jax.random.split(jax.random.fold_in(arg_keys[9], part), 10)
    return {
        "tokens": gaussian(part_keys[0], (VIEWS, TOK_VIEW, D), 1.0, 6.0, ((0, 16),)),
        "in_gain": draw_in_gain(jax.random.fold_in(arg_keys[9], 71), part),
        "w_query": gaussian(arg_keys[2], (D, D), D ** -0.5, 0.1875),
        "w_key": gaussian(arg_keys[3], (D, D), D ** -0.5, 0.1875),
        "w_value": gaussian(arg_keys[4], (D, D), D ** -0.5, 0.1875),
        "w_out": gaussian(arg_keys[5], (D, D), D ** -0.5, 0.1875),
        "out_gain": jnp.clip(1.0 + 0.18 * jax.random.normal(arg_keys[6], (D,), jnp.float32), 0.1, 1.9),
        "covis_list": draw_covis_list(jax.random.fold_in(jax.random.fold_in(arg_keys[9], part), 71), part),
        "covis_count": draw_covis_count(jax.random.fold_in(jax.random.fold_in(arg_keys[9], part), 71), part),
    }


def rms_scale(values, gain):
    mean_sq = lax.optimization_barrier(jnp.mean(values * values, axis=-1, keepdims=True))
    return values * lax.rsqrt(mean_sq + 1e-06) * gain

def reference(tokens, in_gain, w_query, w_key, w_value, w_out, out_gain, covis_list, covis_count):
    normed = rms_scale(tokens.astype(jnp.float32), in_gain).astype(jnp.bfloat16)
    flat = normed.reshape(VIEWS * TOK_VIEW, D)
    query = jnp.dot(flat, w_query, preferred_element_type=jnp.float32).astype(jnp.bfloat16).reshape(VIEWS, TOK_VIEW, HEADS, HEAD_DIM)
    keys = jnp.dot(flat, w_key, preferred_element_type=jnp.float32).astype(jnp.bfloat16).reshape(VIEWS, TOK_VIEW, HEADS, HEAD_DIM)
    values = jnp.dot(flat, w_value, preferred_element_type=jnp.float32).astype(jnp.bfloat16).reshape(VIEWS, TOK_VIEW, HEADS, HEAD_DIM)
    offsets = jnp.arange(-REACH, REACH + 1, dtype=jnp.int32)
    slots = jnp.arange(MAXCOV, dtype=jnp.int32)
    scale = HEAD_DIM ** (-0.5)
    gain_heads = out_gain.reshape(HEADS, HEAD_DIM)

    def one_view(view):
        others = ((view + offsets) % VIEWS).astype(jnp.int32)
        valid = slots < covis_count[view]
        listed = jnp.any((covis_list[view][None, :] == others[:, None]) & valid[None, :], axis=1) | (offsets == 0)
        key_set = keys[others].reshape(-1, HEADS, HEAD_DIM).astype(jnp.float32)
        value_set = values[others].reshape(-1, HEADS, HEAD_DIM).astype(jnp.float32)
        scores = jnp.einsum('qhd,khd->qhk', query[view].astype(jnp.float32), key_set) * scale
        live = jnp.repeat(listed, TOK_VIEW)
        scores = jnp.where(live[None, None, :], scores, -jnp.inf)
        peak = lax.optimization_barrier(jnp.max(scores, axis=-1, keepdims=True))
        weights = jnp.exp(scores - peak)
        total = lax.optimization_barrier(jnp.sum(weights, axis=-1))
        numer = jnp.einsum('qhk,khd->qhd', weights.astype(jnp.bfloat16).astype(jnp.float32), value_set)
        attended = numer / total[..., None]
        head_normed = rms_scale(attended, gain_heads).astype(jnp.bfloat16).reshape(TOK_VIEW, D)
        update = jnp.dot(head_normed, w_out, preferred_element_type=jnp.float32)
        return (tokens[view].astype(jnp.float32) + update).astype(jnp.bfloat16)
    return lax.map(one_view, jnp.arange(VIEWS, dtype=jnp.int32))
```

```python
import functools

import jax
import jax.numpy as jnp
from jax import lax
from jax.experimental import pallas as pl
from jax.experimental.pallas import tpu as pltpu
from jax.sharding import PartitionSpec as P

HEADS = 16
HEAD_DIM = 64
REACH = 6
SPAN = REACH // 2
SLOTS = 2 * SPAN + 2
RELAY = SLOTS - 1
PARTS = 4
ROUNDS = SPAN * PARTS
MESH = pl.DeviceIdType.MESH
INF = float("inf")
LOW = -3e38


def is_grid(chips):
    return chips == 2 * SPAN + 2


def grid_chip(chip, mirror, depth, side):
    z, y = chip // 2, chip % 2
    if depth:
        z = z + 1 - 2 * (z % 2)
    if mirror:
        z = 3 - z
    if side:
        y = 1 - y
    return 2 * z + y


OUTER_SLOTS = ((0, 0, 0), (0, 1, 0), (0, 0, 1), (1, 0, 0), (0, 1, 1), (1, 1, 1), (1, 0, 1))
INNER_SLOTS = ((0, 0, 0), (0, 1, 0), (0, 0, 1), (0, 1, 1), (1, 1, 1), (1, 0, 1), (1, 0, 0))
INNER_STEPS = ((0, 0, 0, 1), (2, 0, 2, 1), (1, 0, 4, 0), (1, 1, 4, 1), (5, 0, 5, 1), (3, 0, 6, 0), (3, 1, 6, 1))
OUTER_STEPS = ((0, 0, 0, 1),) + tuple(
    (1 + 2 * group, late, 2 + 2 * group, late) for group in range(SPAN) for late in range(2)
)


def slot_chips(chip, chips):
    if is_grid(chips):
        outer = (chip // 2) % 3 == 0
        return [
            jnp.where(outer, grid_chip(chip, *far), grid_chip(chip, *near))
            for far, near in zip(OUTER_SLOTS, INNER_SLOTS)
        ]
    found = [chip]
    for hops in range(1, SPAN + 1):
        found += [(chip - hops + chips) % chips, (chip + hops) % chips]
    return found


def body(
    views, tok_hbm, in_gain_hbm, wq_hbm, wk_hbm, wv_hbm, wo_hbm, out_gain_hbm, list_hbm, count_hbm,
    out_ref,
    buf, other, wq, wk, wv, wo, in_gain, out_gain, lists, counts, qpad, kbuf, vtbuf, stats, acc, mask,
    stats_in, acc_in,
    load_sem, send_sem, recv_sem, misc_send, misc_recv,
):
    chips = views // 2
    grid = is_grid(chips)
    me = lax.axis_index("views")
    chip, core = me // 2, me % 2
    partner = chip * 2 + 1 - core
    rows, width = tok_hbm.shape
    heads = width // HEAD_DIM
    size = rows // PARTS
    half = rows // 2
    steps = ROUNDS // 2

    loads = [
        pltpu.make_async_copy(tok_hbm, buf.at[0], load_sem.at[0]),
        pltpu.make_async_copy(in_gain_hbm, in_gain, load_sem.at[5]),
        pltpu.make_async_copy(list_hbm, lists.at[0], load_sem.at[7]),
        pltpu.make_async_copy(count_hbm, counts.at[0], load_sem.at[8]),
        pltpu.make_async_copy(wq_hbm, wq, load_sem.at[1]),
        pltpu.make_async_copy(wk_hbm, wk, load_sem.at[2]),
        pltpu.make_async_copy(wv_hbm, wv, load_sem.at[3]),
        pltpu.make_async_copy(out_gain_hbm, out_gain, load_sem.at[6]),
        pltpu.make_async_copy(wo_hbm, wo, load_sem.at[4]),
    ]

    if grid:
        outer = (chip // 2) % 3 == 0
        beside = grid_chip(chip, 0, 0, 1) * 2 + core
        along = grid_chip(chip, 0, 1, 0) * 2 + core
        across = grid_chip(chip, 1, 0, 0) * 2 + core
        skip = grid_chip(chip, 1, 1, 0) * 2 + core
    else:
        outer = None
        beside = (chip + chips - 1) % chips * 2 + core
        along = (chip + 1) % chips * 2 + core

    barrier = pltpu.get_barrier_semaphore()
    for device in (partner, beside, along):
        pl.semaphore_signal(barrier, inc=1, device_id={"views": device}, device_id_type=MESH)
    if grid:
        @pl.when(jnp.logical_not(outer))
        def _():
            for device in (across, skip):
                pl.semaphore_signal(barrier, inc=1, device_id={"views": device}, device_id_type=MESH)
    for load in loads:
        load.start()
    pl.semaphore_wait(barrier, 4 if grid else 3)

    def send(kind, source, slot, part, device):
        span = pl.ds(pl.multiple_of(part * size, size), size)
        return pltpu.make_async_remote_copy(
            src_ref=tok_hbm.at[span] if source is None else buf.at[source, span],
            dst_ref=buf.at[slot, span],
            send_sem=send_sem.at[kind, part],
            recv_sem=recv_sem.at[slot, part],
            device_id={"views": device},
            device_id_type=MESH,
        )

    def arrived(slot, part):
        send(0, slot, slot, part, partner).wait_recv()

    def partner_copy(src, dst, index):
        return pltpu.make_async_remote_copy(
            src_ref=src, dst_ref=dst, send_sem=misc_send.at[index], recv_sem=misc_recv.at[index],
            device_id={"views": partner}, device_id_type=MESH,
        )

    first_copies = [
        partner_copy(tok_hbm, other, 0),
        partner_copy(list_hbm, lists.at[1], 1),
        partner_copy(count_hbm, counts.at[1], 2),
    ]
    if grid:
        @pl.when(outer)
        def _():
            for part in range(PARTS):
                send(0, None, RELAY, part, skip).start()
                send(2, None, 2, part, beside).start()
            for part in range(PARTS):
                send(1, None, 1, part, along).start()

        @pl.when(jnp.logical_not(outer))
        def _():
            for part in range(PARTS):
                send(0, None, 1, part, along).start()
                send(1, None, 2, part, beside).start()
    else:
        for part in range(PARTS):
            send(0, None, 1, part, along).start()
            send(1, None, 2, part, beside).start()
    for copy in first_copies:
        copy.start()

    def ring_poll(r):
        group, part = r // PARTS, r % PARTS
        arrived(1 + 2 * group, part)
        arrived(2 + 2 * group, part)

        @pl.when(group < SPAN - 1)
        def _():
            send(2 + 2 * group, 1 + 2 * group, 3 + 2 * group, part, along).start()
            send(3 + 2 * group, 2 + 2 * group, 4 + 2 * group, part, beside).start()

    def outer_poll(r):
        group, part = r // PARTS, r % PARTS
        arrived(1 + 2 * group, part)

        @pl.when(group < 2)
        def _():
            send(3 + group, 1 + 2 * group, 4 + 2 * group, part, beside).start()
        arrived(2 + 2 * group, part)

        @pl.when(group == 0)
        def _():
            send(5, 2, 3, part, along).start()

    def far_on(part):
        arrived(RELAY, part)
        send(3, RELAY, 3, part, along).start()
        send(4, RELAY, 4, part, beside).start()

    def corner_on(part):
        arrived(5, part)
        send(5, 5, 5, part, along).start()

    def inner_poll(r):
        if r < PARTS:
            arrived(2, r)
        if 1 <= r < 5:
            far_on(r - 1)
        if r == 2:
            for part in range(3):
                send(6, 2, 5, part, across).start()
        if r == 3:
            send(6, 2, 5, 3, across).start()
            for part in range(PARTS):
                send(2, None, 6, part, across).start()
        if 5 <= r < 9:
            corner_on(r - 5)
        if 4 <= r < 8:
            arrived(1, r - 4)
            arrived(4, r - 4)
        if 8 <= r < 12:
            arrived(3, r - 8)
        if 9 <= r:
            arrived(6, r - 9)

    inner_polls = {
        0: ((0,), (1, 2, 3)), 1: ((4,), (5,)), 2: ((6,), (7,)), 3: ((8,), ()), 4: ((9,), (10,)), 5: ((11,), (12,)),
    }

    def poll(j, second):
        if not grid:
            @pl.when(j < steps)
            def _():
                ring_poll(2 * j + second)
            return

        @pl.when(jnp.logical_and(outer, j < steps))
        def _():
            outer_poll(2 * j + second)

        @pl.when(jnp.logical_not(outer))
        def _():
            for at, polls in inner_polls.items():
                if polls[second]:
                    @pl.when(j == at)
                    def _(polls=polls):
                        for r in polls[second]:
                            inner_poll(r)

    stats[:, 0] = jnp.full((heads, 2 * rows), LOW, jnp.float32)
    stats[:, 1] = jnp.zeros((heads, 2 * rows), jnp.float32)
    acc[...] = jnp.zeros(acc.shape, jnp.float32)
    for load in loads[:4]:
        load.wait()

    def normed_of(raw):
        raw = raw.astype(jnp.float32)
        mean_sq = jnp.mean(raw * raw, axis=-1, keepdims=True)
        return (raw * lax.rsqrt(mean_sq + 1e-6) * in_gain[...]).astype(jnp.bfloat16)

    for copy in first_copies:
        copy.wait_recv()
    ids = jnp.zeros((8, 1), jnp.int32)
    line = lax.broadcasted_iota(jnp.int32, (8, 1), 0)
    for slot, at in enumerate(slot_chips(chip, chips)):
        ids = jnp.where(line == slot, at * 2 + core, ids)
    for side, query_view in enumerate((me, partner)):
        listed = lists[side]
        valid = lax.broadcasted_iota(jnp.int32, (8, listed.shape[1]), 1) < counts[side:side + 1, :]
        hits = jnp.where(((listed == ids) | (ids == query_view)) & valid, 1.0, 0.0)
        mask[:, side * rows:(side + 1) * rows] = jnp.broadcast_to(
            jnp.max(hits, axis=1, keepdims=True), (8, rows)
        )

    loads[4].wait()
    query_in = jnp.concatenate([normed_of(buf[0]), normed_of(other[...])], axis=0)
    query = jnp.dot(query_in, wq[...], preferred_element_type=jnp.float32).astype(jnp.bfloat16)
    query = query.astype(jnp.float32) * HEAD_DIM ** (-0.5)
    query_t = query.T.astype(jnp.bfloat16)
    zero = jnp.zeros((HEAD_DIM, 2 * rows), jnp.bfloat16)
    for h in range(heads):
        mine = query_t[h * HEAD_DIM:(h + 1) * HEAD_DIM, :]
        qpad[h] = jnp.concatenate([mine, zero] if h % 2 == 0 else [zero, mine], axis=0)
    loads[5].wait()
    loads[6].wait()

    def project(first, second):
        normed = normed_of(jnp.concatenate([first, second], axis=0))
        kbuf[...] = jnp.dot(normed, wk[...], preferred_element_type=jnp.float32).astype(jnp.bfloat16)
        value = jnp.dot(normed, wv[...], preferred_element_type=jnp.float32)
        vtbuf[...] = value.T.astype(jnp.bfloat16)

    def attend(near, far):
        on_first = mask[pl.ds(near, 1), :] > 0.5
        on_second = mask[pl.ds(far, 1), :] > 0.5
        keys = kbuf.shape[0] // 2

        def scores_of(h):
            pair = (h // 2) * 2 * HEAD_DIM
            return jnp.dot(kbuf[:, pair:pair + 2 * HEAD_DIM], qpad[h], preferred_element_type=jnp.float32)

        def finish(p):
            h, keep, weights = p
            feats = slice(h * HEAD_DIM, (h + 1) * HEAD_DIM)
            acc[feats, :] = acc[feats, :] * keep + jnp.dot(vtbuf[feats, :], weights, preferred_element_type=jnp.float32)

        waiting = scores_of(0)
        pend = None
        for h in range(heads):
            scores = waiting
            if h + 1 < heads:
                waiting = scores_of(h + 1)
            first, second = scores[:keys], scores[keys:]
            old = stats[h, 0:1, :]
            new = jnp.maximum(
                jnp.where(on_first, jnp.max(first, axis=0, keepdims=True), -INF),
                jnp.where(on_second, jnp.max(second, axis=0, keepdims=True), -INF),
            )
            new = jnp.maximum(old, new)
            e_first = jnp.exp(first - jnp.where(on_first, new, INF))
            e_second = jnp.exp(second - jnp.where(on_second, new, INF))
            keep = jnp.exp(old - new)
            stats[h, 0:1, :] = new
            stats[h, 1:2, :] = stats[h, 1:2, :] * keep + jnp.sum(e_first + e_second, axis=0, keepdims=True)
            weights = jnp.concatenate([e_first.astype(jnp.bfloat16), e_second.astype(jnp.bfloat16)], axis=0)
            if pend is not None:
                finish(pend)
            pend = (h, keep, weights)
        finish(pend)

    def pick(table, j):
        found = table[0]
        for at in range(1, len(table)):
            found = jnp.where(j == at, table[at], found)
        return found

    def step(j, carry):
        if grid:
            picks = [
                jnp.where(outer, pick(far, j), pick(near, j))
                for far, near in zip(zip(*OUTER_STEPS), zip(*INNER_STEPS))
            ]
        else:
            picks = [pick(column, j) for column in zip(*OUTER_STEPS)]
        near, near_half, far, far_half = picks
        near_row = pl.multiple_of(near_half * half, half)
        far_row = pl.multiple_of(far_half * half, half)
        project(buf[near, pl.ds(near_row, half)], buf[far, pl.ds(far_row, half)])
        poll(j, 0)
        attend(near, far)
        poll(j, 1)
        return carry

    lax.fori_loop(0, steps + 1, step, 0)

    swaps = [
        partner_copy(stats.at[:, :, pl.ds(rows, rows)], stats_in, 3),
        partner_copy(acc.at[:, pl.ds(rows, rows)], acc_in, 4),
    ]
    for swap in swaps:
        swap.start()
    loads[7].wait()
    loads[8].wait()
    for swap in swaps:
        swap.wait_recv()
    gain = out_gain[...]
    pieces = []
    for h in range(heads):
        feats = slice(h * HEAD_DIM, (h + 1) * HEAD_DIM)
        peak, peak_in = stats[h, 0:1, :rows], stats_in[h, 0:1, :]
        new = jnp.maximum(peak, peak_in)
        keep, keep_in = jnp.exp(peak - new), jnp.exp(peak_in - new)
        total = stats[h, 1:2, :rows] * keep + stats_in[h, 1:2, :] * keep_in
        attended = (acc[feats, :rows] * keep + acc_in[feats, :] * keep_in) / total
        mean_sq = jnp.mean(attended * attended, axis=0, keepdims=True)
        pieces.append(attended * lax.rsqrt(mean_sq + 1e-6))
    head_normed = (jnp.concatenate(pieces, axis=0).T * gain).astype(jnp.bfloat16)
    update = jnp.dot(head_normed, wo[...], preferred_element_type=jnp.float32)
    out_ref[...] = (buf[0].astype(jnp.float32) + update).astype(out_ref.dtype)

    for part in range(PARTS):
        for kind in range(6):
            send(kind, None, 1, part, partner).wait_send()
        if grid:
            @pl.when(jnp.logical_not(outer))
            def _(part=part):
                send(6, None, 1, part, partner).wait_send()
    for copy in first_copies + swaps:
        copy.wait_send()


def on_device(tokens, in_gain, w_query, w_key, w_value, w_out, out_gain, covis_list, covis_count):
    views = lax.axis_size("views")
    rows, width = tokens.shape[1:]
    slots_listed = covis_list.shape[1]
    hbm = pl.BlockSpec(memory_space=pltpu.HBM)
    vmem = pl.BlockSpec(memory_space=pltpu.VMEM)
    bf16, f32 = jnp.bfloat16, jnp.float32
    heads = width // HEAD_DIM
    dma = pltpu.SemaphoreType.DMA
    out = pl.pallas_call(
        functools.partial(body, views),
        out_shape=jax.ShapeDtypeStruct((rows, width), tokens.dtype),
        in_specs=[hbm] * 9,
        out_specs=vmem,
        scratch_shapes=[
            pltpu.VMEM((SLOTS, rows, width), bf16),
            pltpu.VMEM((rows, width), bf16),
            pltpu.VMEM((width, width), bf16),
            pltpu.VMEM((width, width), bf16),
            pltpu.VMEM((width, width), bf16),
            pltpu.VMEM((width, width), bf16),
            pltpu.VMEM((1, width), f32),
            pltpu.VMEM((1, width), f32),
            pltpu.VMEM((2, 1, slots_listed), jnp.int32),
            pltpu.VMEM((2, 1), jnp.int32),
            pltpu.VMEM((heads, 2 * HEAD_DIM, 2 * rows), bf16),
            pltpu.VMEM((rows, width), bf16),
            pltpu.VMEM((width, rows), bf16),
            pltpu.VMEM((heads, 2, 2 * rows), f32),
            pltpu.VMEM((width, 2 * rows), f32),
            pltpu.VMEM((8, 2 * rows), f32),
            pltpu.VMEM((heads, 2, rows), f32),
            pltpu.VMEM((width, rows), f32),
            dma((9,)),
            dma((8, PARTS)),
            dma((SLOTS, PARTS)),
            dma((5,)),
            dma((5,)),
        ],
        compiler_params=pltpu.CompilerParams(
            collective_id=0, has_side_effects=True, vmem_limit_bytes=60 * 1024 * 1024
        ),
    )(tokens[0], in_gain[None], w_query, w_key, w_value, w_out, out_gain[None], covis_list, covis_count)
    return out[None]


def solution(mesh):
    in_specs = (
        P(("groups", "views"), None, None),
        P(), P(), P(), P(), P(), P(),
        P(("groups", "views"), None),
        P(("groups", "views")),
    )
    out_specs = P(("groups", "views"), None, None)
    return jax.shard_map(on_device, mesh=mesh, in_specs=in_specs, out_specs=out_specs, check_vma=False)
```

```python
import functools

import jax
import jax.numpy as jnp
from jax import lax
from jax.experimental import pallas as pl
from jax.experimental.pallas import tpu as pltpu
from jax.sharding import PartitionSpec as P

HEADS = 16
HEAD_DIM = 64
REACH = 6
SPAN = REACH // 2
SLOTS = 2 * SPAN + 2
RELAY = SLOTS - 1
PARTS = 4
ROUNDS = SPAN * PARTS
GROUP = 4
MESH = pl.DeviceIdType.MESH
INF = float("inf")
LOW = -3e38


def is_grid(chips):
    return chips == 2 * SPAN + 2


def grid_chip(chip, mirror, depth, side):
    z, y = chip // 2, chip % 2
    if depth:
        z = z + 1 - 2 * (z % 2)
    if mirror:
        z = 3 - z
    if side:
        y = 1 - y
    return 2 * z + y


OUTER_SLOTS = ((0, 0, 0), (0, 1, 0), (0, 0, 1), (1, 0, 0), (0, 1, 1), (1, 1, 1), (1, 0, 1))
INNER_SLOTS = ((0, 0, 0), (0, 1, 0), (0, 0, 1), (0, 1, 1), (1, 1, 1), (1, 0, 1), (1, 0, 0))
INNER_STEPS = ((0, 0, 0, 1), (2, 0, 2, 1), (1, 0, 4, 0), (1, 1, 4, 1), (5, 0, 5, 1), (3, 0, 6, 0), (3, 1, 6, 1))
OUTER_STEPS = ((0, 0, 0, 1),) + tuple(
    (1 + 2 * group, late, 2 + 2 * group, late) for group in range(SPAN) for late in range(2)
)


def slot_chips(chip, chips):
    if is_grid(chips):
        outer = (chip // 2) % 3 == 0
        return [
            jnp.where(outer, grid_chip(chip, *far), grid_chip(chip, *near))
            for far, near in zip(OUTER_SLOTS, INNER_SLOTS)
        ]
    found = [chip]
    for hops in range(1, SPAN + 1):
        found += [(chip - hops + chips) % chips, (chip + hops) % chips]
    return found


def body(
    views, tok_hbm, in_gain_hbm, wq_hbm, wk_hbm, wv_hbm, wo_hbm, out_gain_hbm, list_hbm, count_hbm,
    out_ref,
    buf, other, wq, wk, wv, wo, in_gain, out_gain, lists, counts, qpad, kbuf, vtbuf,
    peaks, totals, acc, mask, stats_out, stats_in, acc_in,
    load_sem, send_sem, recv_sem, misc_send, misc_recv,
):
    chips = views // 2
    grid = is_grid(chips)
    me = lax.axis_index("views")
    chip, core = me // 2, me % 2
    partner = chip * 2 + 1 - core
    rows, width = tok_hbm.shape
    heads = width // HEAD_DIM
    size = rows // PARTS
    half = rows // 2
    steps = ROUNDS // 2
    groups = heads // GROUP

    loads = [
        pltpu.make_async_copy(tok_hbm, buf.at[0], load_sem.at[0]),
        pltpu.make_async_copy(in_gain_hbm, in_gain, load_sem.at[5]),
        pltpu.make_async_copy(list_hbm, lists.at[0], load_sem.at[7]),
        pltpu.make_async_copy(count_hbm, counts.at[0], load_sem.at[8]),
        pltpu.make_async_copy(wq_hbm, wq, load_sem.at[1]),
        pltpu.make_async_copy(wk_hbm, wk, load_sem.at[2]),
        pltpu.make_async_copy(wv_hbm, wv, load_sem.at[3]),
        pltpu.make_async_copy(out_gain_hbm, out_gain, load_sem.at[6]),
        pltpu.make_async_copy(wo_hbm, wo, load_sem.at[4]),
    ]

    if grid:
        outer = (chip // 2) % 3 == 0
        beside = grid_chip(chip, 0, 0, 1) * 2 + core
        along = grid_chip(chip, 0, 1, 0) * 2 + core
        across = grid_chip(chip, 1, 0, 0) * 2 + core
        skip = grid_chip(chip, 1, 1, 0) * 2 + core
    else:
        outer = None
        beside = (chip + chips - 1) % chips * 2 + core
        along = (chip + 1) % chips * 2 + core

    barrier = pltpu.get_barrier_semaphore()
    for device in (partner, beside, along):
        pl.semaphore_signal(barrier, inc=1, device_id={"views": device}, device_id_type=MESH)
    if grid:
        @pl.when(jnp.logical_not(outer))
        def _():
            for device in (across, skip):
                pl.semaphore_signal(barrier, inc=1, device_id={"views": device}, device_id_type=MESH)
    for load in loads:
        load.start()
    pl.semaphore_wait(barrier, 4 if grid else 3)

    def send(kind, source, slot, part, device):
        span = pl.ds(pl.multiple_of(part * size, size), size)
        return pltpu.make_async_remote_copy(
            src_ref=tok_hbm.at[span] if source is None else buf.at[source, span],
            dst_ref=buf.at[slot, span],
            send_sem=send_sem.at[kind, part],
            recv_sem=recv_sem.at[slot, part],
            device_id={"views": device},
            device_id_type=MESH,
        )

    def arrived(slot, part):
        send(0, slot, slot, part, partner).wait_recv()

    def partner_copy(src, dst, index):
        return pltpu.make_async_remote_copy(
            src_ref=src, dst_ref=dst, send_sem=misc_send.at[index], recv_sem=misc_recv.at[index],
            device_id={"views": partner}, device_id_type=MESH,
        )

    first_copies = [
        partner_copy(tok_hbm, other, 0),
        partner_copy(list_hbm, lists.at[1], 1),
        partner_copy(count_hbm, counts.at[1], 2),
    ]
    if grid:
        @pl.when(outer)
        def _():
            for part in range(PARTS):
                send(0, None, RELAY, part, skip).start()
                send(2, None, 2, part, beside).start()
            for part in range(PARTS):
                send(1, None, 1, part, along).start()

        @pl.when(jnp.logical_not(outer))
        def _():
            for part in range(PARTS):
                send(0, None, 1, part, along).start()
                send(1, None, 2, part, beside).start()
    else:
        for part in range(PARTS):
            send(0, None, 1, part, along).start()
            send(1, None, 2, part, beside).start()
    for copy in first_copies:
        copy.start()

    def ring_poll(r):
        group, part = r // PARTS, r % PARTS
        arrived(1 + 2 * group, part)
        arrived(2 + 2 * group, part)

        @pl.when(group < SPAN - 1)
        def _():
            send(2 + 2 * group, 1 + 2 * group, 3 + 2 * group, part, along).start()
            send(3 + 2 * group, 2 + 2 * group, 4 + 2 * group, part, beside).start()

    def outer_poll(r):
        group, part = r // PARTS, r % PARTS
        arrived(1 + 2 * group, part)

        @pl.when(group < 2)
        def _():
            send(3 + group, 1 + 2 * group, 4 + 2 * group, part, beside).start()
        arrived(2 + 2 * group, part)

        @pl.when(group == 0)
        def _():
            send(5, 2, 3, part, along).start()

    def far_on(part):
        arrived(RELAY, part)
        send(3, RELAY, 3, part, along).start()
        send(4, RELAY, 4, part, beside).start()

    def corner_on(part):
        arrived(5, part)
        send(5, 5, 5, part, along).start()

    def inner_poll(r):
        if r < PARTS:
            arrived(2, r)
        if 1 <= r < 5:
            far_on(r - 1)
        if r == 2:
            for part in range(3):
                send(6, 2, 5, part, across).start()
        if r == 3:
            send(6, 2, 5, 3, across).start()
            for part in range(PARTS):
                send(2, None, 6, part, across).start()
        if 5 <= r < 9:
            corner_on(r - 5)
        if 4 <= r < 8:
            arrived(1, r - 4)
            arrived(4, r - 4)
        if 8 <= r < 12:
            arrived(3, r - 8)
        if 9 <= r:
            arrived(6, r - 9)

    inner_polls = {
        0: ((0,), (1, 2, 3)), 1: ((4,), (5,)), 2: ((6,), (7,)), 3: ((8,), ()), 4: ((9,), (10,)), 5: ((11,), (12,)),
    }

    def poll(j, second):
        ahead = j < steps
        if not grid:
            @pl.when(ahead)
            def _():
                ring_poll(2 * j + second)
            return

        @pl.when(jnp.logical_and(outer, ahead))
        def _():
            outer_poll(2 * j + second)

        @pl.when(jnp.logical_not(outer))
        def _():
            for at, polls in inner_polls.items():
                if polls[second]:
                    @pl.when(j == at)
                    def _(polls=polls):
                        for r in polls[second]:
                            inner_poll(r)

    peaks[...] = jnp.full(peaks.shape, LOW, jnp.float32)
    totals[...] = jnp.zeros(totals.shape, jnp.float32)
    acc[...] = jnp.zeros(acc.shape, jnp.float32)
    for load in loads[:4]:
        load.wait()

    def normed_of(raw):
        raw = raw.astype(jnp.float32)
        mean_sq = jnp.mean(raw * raw, axis=-1, keepdims=True)
        return (raw * lax.rsqrt(mean_sq + 1e-6) * in_gain[...]).astype(jnp.bfloat16)

    for copy in first_copies:
        copy.wait_recv()
    ids = jnp.zeros((8, 1), jnp.int32)
    line = lax.broadcasted_iota(jnp.int32, (8, 1), 0)
    for slot, at in enumerate(slot_chips(chip, chips)):
        ids = jnp.where(line == slot, at * 2 + core, ids)
    for side, query_view in enumerate((me, partner)):
        listed = lists[side]
        valid = lax.broadcasted_iota(jnp.int32, (8, listed.shape[1]), 1) < counts[side:side + 1, :]
        hits = jnp.where(((listed == ids) | (ids == query_view)) & valid, 1.0, 0.0)
        hit = jnp.max(hits, axis=1, keepdims=True)
        for slot in range(SLOTS):
            mask[slot, :, side * rows:(side + 1) * rows] = jnp.broadcast_to(hit[slot:slot + 1], (8, rows))

    loads[4].wait()
    query_in = jnp.concatenate([normed_of(buf[0]), normed_of(other[...])], axis=0)
    query = jnp.dot(query_in, wq[...], preferred_element_type=jnp.float32).astype(jnp.bfloat16)
    query = query.astype(jnp.float32) * HEAD_DIM ** (-0.5)
    query_t = query.T.astype(jnp.bfloat16)
    zero = jnp.zeros((HEAD_DIM, 2 * rows), jnp.bfloat16)
    for h in range(heads):
        mine = query_t[h * HEAD_DIM:(h + 1) * HEAD_DIM, :]
        qpad[h] = jnp.concatenate([mine, zero] if h % 2 == 0 else [zero, mine], axis=0)
    loads[5].wait()
    loads[6].wait()

    def project(first, second, keys, values):
        normed = normed_of(jnp.concatenate([first, second], axis=0))
        keys[...] = jnp.dot(normed, wk[...], preferred_element_type=jnp.float32).astype(jnp.bfloat16)
        value = jnp.dot(normed, wv[...], preferred_element_type=jnp.float32)
        values[...] = value.T.astype(jnp.bfloat16)

    def attend(near, far, keys, values, handed=None):
        on_first, on_second = mask[near] > 0.5, mask[far] > 0.5
        span = keys.shape[0]
        tiles = span // 16
        queries = 2 * rows

        def scores_of(h):
            pair = (h // 2) * 2 * HEAD_DIM
            scores = jnp.dot(keys[:, pair:pair + 2 * HEAD_DIM], qpad[h], preferred_element_type=jnp.float32)
            return scores.reshape(2 * tiles, 8, queries)

        def finish(p):
            h, keep, weights = p
            feats = slice(h * HEAD_DIM, (h + 1) * HEAD_DIM)
            kept = acc[feats, :].reshape(HEAD_DIM // 8, 8, queries) * keep[None]
            acc[feats, :] = kept.reshape(HEAD_DIM, queries) + jnp.dot(
                values[feats, :], weights, preferred_element_type=jnp.float32
            )
            if handed is not None and (h + 1) % GROUP == 0:
                handed(h // GROUP)

        waiting = scores_of(0)
        pend = None
        for h in range(heads):
            scores = waiting
            if h + 1 < heads:
                waiting = scores_of(h + 1)
            first, second = scores[:tiles], scores[tiles:]
            old = peaks[h]
            new = jnp.maximum(
                jnp.where(on_first, jnp.max(first, axis=0), -INF),
                jnp.where(on_second, jnp.max(second, axis=0), -INF),
            )
            new = jnp.maximum(old, jnp.broadcast_to(jnp.max(new, axis=0, keepdims=True), (8, queries)))
            e_first = jnp.exp(first - jnp.where(on_first, new, INF)[None])
            e_second = jnp.exp(second - jnp.where(on_second, new, INF)[None])
            keep = jnp.exp(old - new)
            peaks[h] = new
            totals[h] = totals[h] * keep + (jnp.sum(e_first, axis=0) + jnp.sum(e_second, axis=0))
            weights = jnp.concatenate([e_first, e_second], axis=0).reshape(span, queries).astype(jnp.bfloat16)
            if pend is not None:
                finish(pend)
            pend = (h, keep, weights)
        finish(pend)

    def pick(table, j):
        found = table[0]
        for at in range(1, len(table)):
            found = jnp.where(j == at, table[at], found)
        return found

    def step(j, carry):
        if grid:
            picks = [
                jnp.where(outer, pick(far, j), pick(near, j))
                for far, near in zip(zip(*OUTER_STEPS), zip(*INNER_STEPS))
            ]
        else:
            picks = [pick(column, j) for column in zip(*OUTER_STEPS)]
        near, near_half, far, far_half = picks
        near_row = pl.multiple_of(near_half * half, half)
        far_row = pl.multiple_of(far_half * half, half)
        project(buf[near, pl.ds(near_row, half)], buf[far, pl.ds(far_row, half)], kbuf, vtbuf)
        poll(j, 0)
        attend(near, far, kbuf, vtbuf)
        poll(j, 1)
        return carry

    lax.fori_loop(0, steps, step, 0)

    def stats_swap(group):
        return partner_copy(stats_out.at[group], stats_in.at[group], 3 + group)

    def acc_swap(group):
        feats = pl.ds(group * GROUP * HEAD_DIM, GROUP * HEAD_DIM)
        return partner_copy(acc.at[feats, pl.ds(rows, rows)], acc_in.at[feats], 3 + groups + group)

    def totals_of(h, side):
        return jnp.sum(totals[h][:, side * rows:(side + 1) * rows], axis=0, keepdims=True)

    def hand(group):
        acc_swap(group).start()
        members = range(group * GROUP, (group + 1) * GROUP)
        stats_out[group] = jnp.concatenate(
            [peaks[h][:1, rows:] for h in members] + [totals_of(h, 1) for h in members], axis=0
        )
        stats_swap(group).start()

    if grid:
        near, far = (jnp.where(outer, OUTER_STEPS[-1][at], INNER_STEPS[-1][at]) for at in (0, 2))
    else:
        near, far = (jnp.int32(OUTER_STEPS[-1][at]) for at in (0, 2))
    span = pl.ds(half, half)
    project(buf[near, span], buf[far, span], kbuf, vtbuf)
    attend(near, far, kbuf, vtbuf, hand)

    loads[7].wait()
    loads[8].wait()
    update = buf[0].astype(jnp.float32)
    for group in range(groups):
        stats_swap(group).wait_recv()
        acc_swap(group).wait_recv()
        pieces = []
        for at, h in enumerate(range(group * GROUP, (group + 1) * GROUP)):
            feats = slice(h * HEAD_DIM, (h + 1) * HEAD_DIM)
            peak, peak_in = peaks[h][:1, :rows], stats_in[group, at:at + 1, :]
            new = jnp.maximum(peak, peak_in)
            keep, keep_in = jnp.exp(peak - new), jnp.exp(peak_in - new)
            total = totals_of(h, 0) * keep + stats_in[group, GROUP + at:GROUP + at + 1, :] * keep_in
            attended = (acc[feats, :rows] * keep + acc_in[feats, :] * keep_in) / total
            mean_sq = jnp.mean(attended * attended, axis=0, keepdims=True)
            pieces.append(attended * lax.rsqrt(mean_sq + 1e-6))
        feats = slice(group * GROUP * HEAD_DIM, (group + 1) * GROUP * HEAD_DIM)
        head_normed = (jnp.concatenate(pieces, axis=0).T * out_gain[:, feats]).astype(jnp.bfloat16)
        update = update + jnp.dot(head_normed, wo[feats, :], preferred_element_type=jnp.float32)
    out_ref[...] = update.astype(out_ref.dtype)

    for part in range(PARTS):
        for kind in range(6):
            send(kind, None, 1, part, partner).wait_send()
        if grid:
            @pl.when(jnp.logical_not(outer))
            def _(part=part):
                send(6, None, 1, part, partner).wait_send()
    for copy in first_copies:
        copy.wait_send()
    for group in range(groups):
        stats_swap(group).wait_send()
        acc_swap(group).wait_send()


def on_device(tokens, in_gain, w_query, w_key, w_value, w_out, out_gain, covis_list, covis_count):
    views = lax.axis_size("views")
    rows, width = tokens.shape[1:]
    slots_listed = covis_list.shape[1]
    hbm = pl.BlockSpec(memory_space=pltpu.HBM)
    vmem = pl.BlockSpec(memory_space=pltpu.VMEM)
    bf16, f32 = jnp.bfloat16, jnp.float32
    heads = width // HEAD_DIM
    dma = pltpu.SemaphoreType.DMA
    out = pl.pallas_call(
        functools.partial(body, views),
        out_shape=jax.ShapeDtypeStruct((rows, width), tokens.dtype),
        in_specs=[hbm] * 9,
        out_specs=vmem,
        scratch_shapes=[
            pltpu.VMEM((SLOTS, rows, width), bf16),
            pltpu.VMEM((rows, width), bf16),
            pltpu.VMEM((width, width), bf16),
            pltpu.VMEM((width, width), bf16),
            pltpu.VMEM((width, width), bf16),
            pltpu.VMEM((width, width), bf16),
            pltpu.VMEM((1, width), f32),
            pltpu.VMEM((1, width), f32),
            pltpu.VMEM((2, 1, slots_listed), jnp.int32),
            pltpu.VMEM((2, 1), jnp.int32),
            pltpu.VMEM((heads, 2 * HEAD_DIM, 2 * rows), bf16),
            pltpu.VMEM((rows, width), bf16),
            pltpu.VMEM((width, rows), bf16),
            pltpu.VMEM((heads, 8, 2 * rows), f32),
            pltpu.VMEM((heads, 8, 2 * rows), f32),
            pltpu.VMEM((width, 2 * rows), f32),
            pltpu.VMEM((SLOTS, 8, 2 * rows), f32),
            pltpu.VMEM((heads // GROUP, 2 * GROUP, rows), f32),
            pltpu.VMEM((heads // GROUP, 2 * GROUP, rows), f32),
            pltpu.VMEM((width, rows), f32),
            dma((9,)),
            dma((8, PARTS)),
            dma((SLOTS, PARTS)),
            dma((3 + 2 * (heads // GROUP),)),
            dma((3 + 2 * (heads // GROUP),)),
        ],
        compiler_params=pltpu.CompilerParams(
            collective_id=0, has_side_effects=True, vmem_limit_bytes=32 * 1024 * 1024
        ),
    )(*(pltpu.with_memory_space_constraint(a, pltpu.HBM) for a in (tokens[0], in_gain[None], w_query, w_key, w_value, w_out, out_gain[None], covis_list)), covis_count)
    return out[None]


def solution(mesh):
    in_specs = (
        P(("groups", "views"), None, None),
        P(), P(), P(), P(), P(), P(),
        P(("groups", "views"), None),
        P(("groups", "views")),
    )
    out_specs = P(("groups", "views"), None, None)
    return jax.shard_map(on_device, mesh=mesh, in_specs=in_specs, out_specs=out_specs, check_vma=False)
```

```python
import functools

import jax
import jax.numpy as jnp
from jax import lax
from jax.experimental import pallas as pl
from jax.experimental.pallas import tpu as pltpu
from jax.sharding import PartitionSpec as P

HEADS = 16
HEAD_DIM = 64
REACH = 6
SPAN = REACH // 2
SLOTS = 2 * SPAN + 2
RELAY = SLOTS - 1
PARTS = 4
ROUNDS = SPAN * PARTS
GROUP = 4
MESH = pl.DeviceIdType.MESH
INF = float("inf")
LOW = -3e38


def is_grid(chips):
    return chips == 2 * SPAN + 2


def grid_chip(chip, mirror, depth, side):
    z, y = chip // 2, chip % 2
    if depth:
        z = z + 1 - 2 * (z % 2)
    if mirror:
        z = 3 - z
    if side:
        y = 1 - y
    return 2 * z + y


OUTER_SLOTS = ((0, 0, 0), (0, 1, 0), (0, 0, 1), (1, 0, 0), (0, 1, 1), (1, 1, 1), (1, 0, 1))
INNER_SLOTS = ((0, 0, 0), (0, 1, 0), (0, 0, 1), (0, 1, 1), (1, 1, 1), (1, 0, 1), (1, 0, 0))
INNER_STEPS = ((0, 0, 0, 1), (2, 0, 2, 1), (1, 0, 4, 0), (1, 1, 4, 1), (5, 0, 5, 1), (3, 0, 6, 0), (3, 1, 6, 1))
OUTER_STEPS = ((0, 0, 0, 1),) + tuple(
    (1 + 2 * group, late, 2 + 2 * group, late) for group in range(SPAN) for late in range(2)
)


def slot_chips(chip, chips):
    if is_grid(chips):
        outer = (chip // 2) % 3 == 0
        return [
            jnp.where(outer, grid_chip(chip, *far), grid_chip(chip, *near))
            for far, near in zip(OUTER_SLOTS, INNER_SLOTS)
        ]
    found = [chip]
    for hops in range(1, SPAN + 1):
        found += [(chip - hops + chips) % chips, (chip + hops) % chips]
    return found


def body(
    views, tok_hbm, in_gain_hbm, wq_hbm, wk_hbm, wv_hbm, wo_hbm, out_gain_hbm, list_hbm, count_hbm,
    out_ref,
    buf, other, wq, wk, wv, wo, in_gain, out_gain, lists, counts, qpad, kbuf, vtbuf,
    peaks, totals, acc, mask, stats_out, stats_in, acc_in,
    s_even, s_odd, w_even, w_odd, keeps,
    load_sem, send_sem, recv_sem, misc_send, misc_recv,
):
    chips = views // 2
    grid = is_grid(chips)
    me = lax.axis_index("views")
    chip, core = me // 2, me % 2
    partner = chip * 2 + 1 - core
    rows, width = tok_hbm.shape
    heads = width // HEAD_DIM
    size = rows // PARTS
    half = rows // 2
    steps = ROUNDS // 2
    groups = heads // GROUP

    loads = [
        pltpu.make_async_copy(tok_hbm, buf.at[0], load_sem.at[0]),
        pltpu.make_async_copy(in_gain_hbm, in_gain, load_sem.at[5]),
        pltpu.make_async_copy(list_hbm, lists.at[0], load_sem.at[7]),
        pltpu.make_async_copy(count_hbm, counts.at[0], load_sem.at[8]),
        pltpu.make_async_copy(wq_hbm, wq, load_sem.at[1]),
        pltpu.make_async_copy(wk_hbm, wk, load_sem.at[2]),
        pltpu.make_async_copy(wv_hbm, wv, load_sem.at[3]),
        pltpu.make_async_copy(out_gain_hbm, out_gain, load_sem.at[6]),
        pltpu.make_async_copy(wo_hbm, wo, load_sem.at[4]),
    ]

    if grid:
        outer = (chip // 2) % 3 == 0
        beside = grid_chip(chip, 0, 0, 1) * 2 + core
        along = grid_chip(chip, 0, 1, 0) * 2 + core
        across = grid_chip(chip, 1, 0, 0) * 2 + core
        skip = grid_chip(chip, 1, 1, 0) * 2 + core
    else:
        outer = None
        beside = (chip + chips - 1) % chips * 2 + core
        along = (chip + 1) % chips * 2 + core

    barrier = pltpu.get_barrier_semaphore()
    for device in (partner, beside, along):
        pl.semaphore_signal(barrier, inc=1, device_id={"views": device}, device_id_type=MESH)
    if grid:
        @pl.when(jnp.logical_not(outer))
        def _():
            for device in (across, skip):
                pl.semaphore_signal(barrier, inc=1, device_id={"views": device}, device_id_type=MESH)
    for load in loads:
        load.start()
    pl.semaphore_wait(barrier, 4 if grid else 3)

    def send(kind, source, slot, part, device):
        span = pl.ds(pl.multiple_of(part * size, size), size)
        return pltpu.make_async_remote_copy(
            src_ref=tok_hbm.at[span] if source is None else buf.at[source, span],
            dst_ref=buf.at[slot, span],
            send_sem=send_sem.at[kind, part],
            recv_sem=recv_sem.at[slot, part],
            device_id={"views": device},
            device_id_type=MESH,
        )

    def arrived(slot, part):
        send(0, slot, slot, part, partner).wait_recv()

    def partner_copy(src, dst, index):
        return pltpu.make_async_remote_copy(
            src_ref=src, dst_ref=dst, send_sem=misc_send.at[index], recv_sem=misc_recv.at[index],
            device_id={"views": partner}, device_id_type=MESH,
        )

    first_copies = [
        partner_copy(tok_hbm, other, 0),
        partner_copy(list_hbm, lists.at[1], 1),
        partner_copy(count_hbm, counts.at[1], 2),
    ]
    if grid:
        @pl.when(outer)
        def _():
            for part in range(PARTS):
                send(0, None, RELAY, part, skip).start()
                send(2, None, 2, part, beside).start()
            for part in range(PARTS):
                send(1, None, 1, part, along).start()

        @pl.when(jnp.logical_not(outer))
        def _():
            for part in range(PARTS):
                send(0, None, 1, part, along).start()
                send(1, None, 2, part, beside).start()
    else:
        for part in range(PARTS):
            send(0, None, 1, part, along).start()
            send(1, None, 2, part, beside).start()
    for copy in first_copies:
        copy.start()

    def ring_poll(r):
        group, part = r // PARTS, r % PARTS
        arrived(1 + 2 * group, part)
        arrived(2 + 2 * group, part)

        @pl.when(group < SPAN - 1)
        def _():
            send(2 + 2 * group, 1 + 2 * group, 3 + 2 * group, part, along).start()
            send(3 + 2 * group, 2 + 2 * group, 4 + 2 * group, part, beside).start()

    def outer_poll(r):
        group, part = r // PARTS, r % PARTS
        arrived(1 + 2 * group, part)

        @pl.when(group < 2)
        def _():
            send(3 + group, 1 + 2 * group, 4 + 2 * group, part, beside).start()
        arrived(2 + 2 * group, part)

        @pl.when(group == 0)
        def _():
            send(5, 2, 3, part, along).start()

    def far_on(part):
        arrived(RELAY, part)
        send(3, RELAY, 3, part, along).start()
        send(4, RELAY, 4, part, beside).start()

    def corner_on(part):
        arrived(5, part)
        send(5, 5, 5, part, along).start()

    def inner_poll(r):
        if r < PARTS:
            arrived(2, r)
        if 1 <= r < 5:
            far_on(r - 1)
        if r == 2:
            for part in range(3):
                send(6, 2, 5, part, across).start()
        if r == 3:
            send(6, 2, 5, 3, across).start()
            for part in range(PARTS):
                send(2, None, 6, part, across).start()
        if 5 <= r < 9:
            corner_on(r - 5)
        if 4 <= r < 8:
            arrived(1, r - 4)
            arrived(4, r - 4)
        if 8 <= r < 12:
            arrived(3, r - 8)
        if 9 <= r:
            arrived(6, r - 9)

    inner_polls = {
        0: ((0,), (1, 2, 3)), 1: ((4,), (5,)), 2: ((6,), (7,)), 3: ((8,), ()), 4: ((9,), (10,)), 5: ((11,), (12,)),
    }

    def poll(j, second):
        ahead = j < steps
        if not grid:
            @pl.when(ahead)
            def _():
                ring_poll(2 * j + second)
            return

        @pl.when(jnp.logical_and(outer, ahead))
        def _():
            outer_poll(2 * j + second)

        @pl.when(jnp.logical_not(outer))
        def _():
            for at, polls in inner_polls.items():
                if polls[second]:
                    @pl.when(j == at)
                    def _(polls=polls):
                        for r in polls[second]:
                            inner_poll(r)

    peaks[...] = jnp.full(peaks.shape, LOW, jnp.float32)
    totals[...] = jnp.zeros(totals.shape, jnp.float32)
    acc[...] = jnp.zeros(acc.shape, jnp.float32)
    for load in loads[:4]:
        load.wait()

    def normed_of(raw):
        raw = raw.astype(jnp.float32)
        mean_sq = jnp.mean(raw * raw, axis=-1, keepdims=True)
        return (raw * lax.rsqrt(mean_sq + 1e-6) * in_gain[...]).astype(jnp.bfloat16)

    for copy in first_copies:
        copy.wait_recv()
    ids = jnp.zeros((8, 1), jnp.int32)
    line = lax.broadcasted_iota(jnp.int32, (8, 1), 0)
    for slot, at in enumerate(slot_chips(chip, chips)):
        ids = jnp.where(line == slot, at * 2 + core, ids)
    for side, query_view in enumerate((me, partner)):
        listed = lists[side]
        valid = lax.broadcasted_iota(jnp.int32, (8, listed.shape[1]), 1) < counts[side:side + 1, :]
        hits = jnp.where(((listed == ids) | (ids == query_view)) & valid, 1.0, 0.0)
        hit = jnp.max(hits, axis=1, keepdims=True)
        for slot in range(SLOTS):
            mask[slot, :, side * rows:(side + 1) * rows] = jnp.broadcast_to(hit[slot:slot + 1], (8, rows))

    loads[4].wait()
    query_in = jnp.concatenate([normed_of(buf[0]), normed_of(other[...])], axis=0)
    query = jnp.dot(query_in, wq[...], preferred_element_type=jnp.float32).astype(jnp.bfloat16)
    query = query.astype(jnp.float32) * HEAD_DIM ** (-0.5)
    query_t = query.T.astype(jnp.bfloat16)
    zero = jnp.zeros((HEAD_DIM, 2 * rows), jnp.bfloat16)
    for h in range(heads):
        mine = query_t[h * HEAD_DIM:(h + 1) * HEAD_DIM, :]
        qpad[h] = jnp.concatenate([mine, zero] if h % 2 == 0 else [zero, mine], axis=0)
    loads[5].wait()
    loads[6].wait()

    queries = 2 * rows
    tiles = rows // 16

    def project(first, second):
        normed = normed_of(jnp.concatenate([first, second], axis=0))
        key = jnp.dot(normed, wk[...], preferred_element_type=jnp.float32).astype(jnp.bfloat16)
        for pair in range(heads // 2):
            kbuf[pair] = key[:, pair * 2 * HEAD_DIM:(pair + 1) * 2 * HEAD_DIM]
        value = jnp.dot(normed, wv[...], preferred_element_type=jnp.float32)
        vtbuf[...] = value.T.astype(jnp.bfloat16).reshape(vtbuf.shape)

    def score(pair, at, scores):
        scores[at] = jnp.dot(kbuf[pair], qpad[2 * pair + at], preferred_element_type=jnp.float32)

    def weigh(pair, at, scores, weights, keep_ref, on_first, on_second):
        h = 2 * pair + at
        found = scores[at].reshape(2 * tiles, 8, queries)
        first, second = found[:tiles], found[tiles:]
        old = peaks[h]
        new = jnp.maximum(
            jnp.where(on_first, jnp.max(first, axis=0), -INF),
            jnp.where(on_second, jnp.max(second, axis=0), -INF),
        )
        new = jnp.maximum(old, jnp.broadcast_to(jnp.max(new, axis=0, keepdims=True), (8, queries)))
        e_first = jnp.exp(first - jnp.where(on_first, new, INF)[None])
        e_second = jnp.exp(second - jnp.where(on_second, new, INF)[None])
        keep = jnp.exp(old - new)
        peaks[h] = new
        keep_ref[at] = keep
        totals[h] = totals[h] * keep + (jnp.sum(e_first, axis=0) + jnp.sum(e_second, axis=0))
        weights[at] = jnp.concatenate([e_first, e_second], axis=0).reshape(rows, queries).astype(jnp.bfloat16)

    def gather(pair, at, weights, keep_ref):
        h = 2 * pair + at
        kept = acc[h].reshape(HEAD_DIM // 8, 8, queries) * keep_ref[at][None]
        acc[h] = kept.reshape(HEAD_DIM, queries) + jnp.dot(
            vtbuf[h], weights[at], preferred_element_type=jnp.float32
        )

    def attend(near, far, handed=None):
        on_first, on_second = mask[near] > 0.5, mask[far] > 0.5
        pairs = heads // 2
        sides = ((s_even, w_even, keeps.at[0]), (s_odd, w_odd, keeps.at[1]))

        def stage(pair, odd, ahead=True, behind=True):
            scores, weights, keep = sides[odd]
            next_scores, last_weights, last_keep = sides[1 - odd]
            for at in range(2):
                if ahead:
                    score(pair + 1, at, next_scores)
                if behind:
                    gather(pair - 1, at, last_weights, last_keep)
                weigh(pair, at, scores, weights, keep, on_first, on_second)

        for at in range(2):
            score(0, at, s_even)
        stage(0, 0, behind=False)
        if handed is None:
            def both(i, carry):
                stage(2 * i + 1, 1)
                stage(2 * i + 2, 0)
                return carry

            lax.fori_loop(0, pairs // 2 - 1, both, 0)
        else:
            for pair in range(1, pairs - 1):
                stage(pair, pair % 2)
                if (pair * 2) % GROUP == 0:
                    handed(pair * 2 // GROUP - 1)
        stage(pairs - 1, 1, ahead=False)
        for at in range(2):
            gather(pairs - 1, at, w_odd, keeps.at[1])
        if handed is not None:
            handed(groups - 1)

    def pick(table, j):
        found = table[0]
        for at in range(1, len(table)):
            found = jnp.where(j == at, table[at], found)
        return found

    def step(j, carry):
        if grid:
            picks = [
                jnp.where(outer, pick(far, j), pick(near, j))
                for far, near in zip(zip(*OUTER_STEPS), zip(*INNER_STEPS))
            ]
        else:
            picks = [pick(column, j) for column in zip(*OUTER_STEPS)]
        near, near_half, far, far_half = picks
        near_row = pl.multiple_of(near_half * half, half)
        far_row = pl.multiple_of(far_half * half, half)
        project(buf[near, pl.ds(near_row, half)], buf[far, pl.ds(far_row, half)])
        poll(j, 0)
        attend(near, far)
        poll(j, 1)
        return carry

    lax.fori_loop(0, steps, step, 0)

    def stats_swap(group):
        return partner_copy(stats_out.at[group], stats_in.at[group], 3 + group)

    def acc_swap(group):
        members = pl.ds(group * GROUP, GROUP)
        return partner_copy(acc.at[members, :, pl.ds(rows, rows)], acc_in.at[members], 3 + groups + group)

    def totals_of(h, side):
        return jnp.sum(totals[h][:, side * rows:(side + 1) * rows], axis=0, keepdims=True)

    def hand(group):
        acc_swap(group).start()
        members = range(group * GROUP, (group + 1) * GROUP)
        stats_out[group] = jnp.concatenate(
            [peaks[h][:1, rows:] for h in members] + [totals_of(h, 1) for h in members], axis=0
        )
        stats_swap(group).start()

    if grid:
        near, far = (jnp.where(outer, OUTER_STEPS[-1][at], INNER_STEPS[-1][at]) for at in (0, 2))
    else:
        near, far = (jnp.int32(OUTER_STEPS[-1][at]) for at in (0, 2))
    span = pl.ds(half, half)
    project(buf[near, span], buf[far, span])
    attend(near, far, hand)

    loads[7].wait()
    loads[8].wait()
    update = buf[0].astype(jnp.float32)
    for group in range(groups):
        stats_swap(group).wait_recv()
        acc_swap(group).wait_recv()
        pieces = []
        for at, h in enumerate(range(group * GROUP, (group + 1) * GROUP)):
            peak, peak_in = peaks[h][:1, :rows], stats_in[group, at:at + 1, :]
            new = jnp.maximum(peak, peak_in)
            keep, keep_in = jnp.exp(peak - new), jnp.exp(peak_in - new)
            total = totals_of(h, 0) * keep + stats_in[group, GROUP + at:GROUP + at + 1, :] * keep_in
            attended = (acc[h, :, :rows] * keep + acc_in[h] * keep_in) / total
            mean_sq = jnp.mean(attended * attended, axis=0, keepdims=True)
            pieces.append(attended * lax.rsqrt(mean_sq + 1e-6))
        feats = slice(group * GROUP * HEAD_DIM, (group + 1) * GROUP * HEAD_DIM)
        head_normed = (jnp.concatenate(pieces, axis=0).T * out_gain[:, feats]).astype(jnp.bfloat16)
        update = update + jnp.dot(head_normed, wo[feats, :], preferred_element_type=jnp.float32)
    out_ref[...] = update.astype(out_ref.dtype)

    for part in range(PARTS):
        for kind in range(6):
            send(kind, None, 1, part, partner).wait_send()
        if grid:
            @pl.when(jnp.logical_not(outer))
            def _(part=part):
                send(6, None, 1, part, partner).wait_send()
    for copy in first_copies:
        copy.wait_send()
    for group in range(groups):
        stats_swap(group).wait_send()
        acc_swap(group).wait_send()


def on_device(tokens, in_gain, w_query, w_key, w_value, w_out, out_gain, covis_list, covis_count):
    views = lax.axis_size("views")
    rows, width = tokens.shape[1:]
    slots_listed = covis_list.shape[1]
    hbm = pl.BlockSpec(memory_space=pltpu.HBM)
    vmem = pl.BlockSpec(memory_space=pltpu.VMEM)
    bf16, f32 = jnp.bfloat16, jnp.float32
    heads = width // HEAD_DIM
    dma = pltpu.SemaphoreType.DMA
    out = pl.pallas_call(
        functools.partial(body, views),
        out_shape=jax.ShapeDtypeStruct((rows, width), tokens.dtype),
        in_specs=[hbm] * 9,
        out_specs=vmem,
        scratch_shapes=[
            pltpu.VMEM((SLOTS, rows, width), bf16),
            pltpu.VMEM((rows, width), bf16),
            pltpu.VMEM((width, width), bf16),
            pltpu.VMEM((width, width), bf16),
            pltpu.VMEM((width, width), bf16),
            pltpu.VMEM((width, width), bf16),
            pltpu.VMEM((1, width), f32),
            pltpu.VMEM((1, width), f32),
            pltpu.VMEM((2, 1, slots_listed), jnp.int32),
            pltpu.VMEM((2, 1), jnp.int32),
            pltpu.VMEM((heads, 2 * HEAD_DIM, 2 * rows), bf16),
            pltpu.VMEM((heads // 2, rows, 2 * HEAD_DIM), bf16),
            pltpu.VMEM((heads, HEAD_DIM, rows), bf16),
            pltpu.VMEM((heads, 8, 2 * rows), f32),
            pltpu.VMEM((heads, 8, 2 * rows), f32),
            pltpu.VMEM((heads, HEAD_DIM, 2 * rows), f32),
            pltpu.VMEM((SLOTS, 8, 2 * rows), f32),
            pltpu.VMEM((heads // GROUP, 2 * GROUP, rows), f32),
            pltpu.VMEM((heads // GROUP, 2 * GROUP, rows), f32),
            pltpu.VMEM((heads, HEAD_DIM, rows), f32),
            pltpu.VMEM((2, rows, 2 * rows), f32),
            pltpu.VMEM((2, rows, 2 * rows), f32),
            pltpu.VMEM((2, rows, 2 * rows), bf16),
            pltpu.VMEM((2, rows, 2 * rows), bf16),
            pltpu.VMEM((2, 2, 8, 2 * rows), f32),
            dma((9,)),
            dma((8, PARTS)),
            dma((SLOTS, PARTS)),
            dma((3 + 2 * (heads // GROUP),)),
            dma((3 + 2 * (heads // GROUP),)),
        ],
        compiler_params=pltpu.CompilerParams(
            collective_id=0, has_side_effects=True, vmem_limit_bytes=32 * 1024 * 1024
        ),
    )(*(pltpu.with_memory_space_constraint(a, pltpu.HBM) for a in (tokens[0], in_gain[None], w_query, w_key, w_value, w_out, out_gain[None], covis_list)), covis_count)
    return out[None]


def solution(mesh):
    in_specs = (
        P(("groups", "views"), None, None),
        P(), P(), P(), P(), P(), P(),
        P(("groups", "views"), None),
        P(("groups", "views")),
    )
    out_specs = P(("groups", "views"), None, None)
    return jax.shard_map(on_device, mesh=mesh, in_specs=in_specs, out_specs=out_specs, check_vma=False)
```

```python
import functools

import jax
import jax.numpy as jnp
from jax import lax
from jax.experimental import pallas as pl
from jax.experimental.pallas import tpu as pltpu
from jax.sharding import PartitionSpec as P

HEADS = 16
HEAD_DIM = 64
REACH = 6
SPAN = REACH // 2
SLOTS = 2 * SPAN + 2
RELAY = SLOTS - 1
PARTS = 4
ROUNDS = SPAN * PARTS
GROUP = 4
MESH = pl.DeviceIdType.MESH
INF = float("inf")
LOW = -3e38


def is_grid(chips):
    return chips == 2 * SPAN + 2


def grid_chip(chip, mirror, depth, side):
    z, y = chip // 2, chip % 2
    if depth:
        z = z + 1 - 2 * (z % 2)
    if mirror:
        z = 3 - z
    if side:
        y = 1 - y
    return 2 * z + y


OUTER_SLOTS = ((0, 0, 0), (0, 1, 0), (0, 0, 1), (1, 0, 0), (0, 1, 1), (1, 1, 1), (1, 0, 1))
INNER_SLOTS = ((0, 0, 0), (0, 1, 0), (0, 0, 1), (0, 1, 1), (1, 1, 1), (1, 0, 1), (1, 0, 0))
INNER_STEPS = ((0, 0, 0, 1), (2, 0, 2, 1), (1, 0, 4, 0), (1, 1, 4, 1), (5, 0, 5, 1), (3, 0, 6, 0), (3, 1, 6, 1))
OUTER_STEPS = ((0, 0, 0, 1),) + tuple(
    (1 + 2 * group, late, 2 + 2 * group, late) for group in range(SPAN) for late in range(2)
)


def slot_chips(chip, chips):
    if is_grid(chips):
        outer = (chip // 2) % 3 == 0
        return [
            jnp.where(outer, grid_chip(chip, *far), grid_chip(chip, *near))
            for far, near in zip(OUTER_SLOTS, INNER_SLOTS)
        ]
    found = [chip]
    for hops in range(1, SPAN + 1):
        found += [(chip - hops + chips) % chips, (chip + hops) % chips]
    return found


def body(
    views, tok_hbm, in_gain_hbm, wq_hbm, wk_hbm, wv_hbm, wo_hbm, out_gain_hbm, list_hbm, count_hbm,
    out_ref,
    buf, other, wq, wk, wv, wo, in_gain, out_gain, lists, counts, qpad, kbuf, vtbuf,
    peaks, totals, acc, mask, stats_out, stats_in, acc_in,
    s_even, s_odd, w_even, w_odd, keeps,
    load_sem, send_sem, recv_sem, misc_send, misc_recv,
):
    chips = views // 2
    grid = is_grid(chips)
    me = lax.axis_index("views")
    chip, core = me // 2, me % 2
    partner = chip * 2 + 1 - core
    rows, width = tok_hbm.shape
    heads = width // HEAD_DIM
    size = rows // PARTS
    half = rows // 2
    steps = ROUNDS // 2
    groups = heads // GROUP

    loads = [
        pltpu.make_async_copy(tok_hbm, buf.at[0], load_sem.at[0]),
        pltpu.make_async_copy(in_gain_hbm, in_gain, load_sem.at[5]),
        pltpu.make_async_copy(list_hbm, lists.at[0], load_sem.at[7]),
        pltpu.make_async_copy(count_hbm, counts.at[0], load_sem.at[8]),
        pltpu.make_async_copy(wq_hbm, wq, load_sem.at[1]),
        pltpu.make_async_copy(wk_hbm, wk, load_sem.at[2]),
        pltpu.make_async_copy(wv_hbm, wv, load_sem.at[3]),
        pltpu.make_async_copy(out_gain_hbm, out_gain, load_sem.at[6]),
        pltpu.make_async_copy(wo_hbm, wo, load_sem.at[4]),
    ]

    if grid:
        outer = (chip // 2) % 3 == 0
        beside = grid_chip(chip, 0, 0, 1) * 2 + core
        along = grid_chip(chip, 0, 1, 0) * 2 + core
        across = grid_chip(chip, 1, 0, 0) * 2 + core
        skip = grid_chip(chip, 1, 1, 0) * 2 + core
    else:
        outer = None
        beside = (chip + chips - 1) % chips * 2 + core
        along = (chip + 1) % chips * 2 + core

    barrier = pltpu.get_barrier_semaphore()
    for device in (partner, beside, along):
        pl.semaphore_signal(barrier, inc=1, device_id={"views": device}, device_id_type=MESH)
    if grid:
        @pl.when(jnp.logical_not(outer))
        def _():
            for device in (across, skip):
                pl.semaphore_signal(barrier, inc=1, device_id={"views": device}, device_id_type=MESH)
    for load in loads:
        load.start()
    pl.semaphore_wait(barrier, 4 if grid else 3)

    def send(kind, source, slot, part, device):
        span = pl.ds(pl.multiple_of(part * size, size), size)
        return pltpu.make_async_remote_copy(
            src_ref=tok_hbm.at[span] if source is None else buf.at[source, span],
            dst_ref=buf.at[slot, span],
            send_sem=send_sem.at[kind, part],
            recv_sem=recv_sem.at[slot, part],
            device_id={"views": device},
            device_id_type=MESH,
        )

    def arrived(slot, part):
        send(0, slot, slot, part, partner).wait_recv()

    def partner_copy(src, dst, index):
        return pltpu.make_async_remote_copy(
            src_ref=src, dst_ref=dst, send_sem=misc_send.at[index], recv_sem=misc_recv.at[index],
            device_id={"views": partner}, device_id_type=MESH,
        )

    first_copies = [
        partner_copy(tok_hbm, other, 0),
        partner_copy(list_hbm, lists.at[1], 1),
        partner_copy(count_hbm, counts.at[1], 2),
    ]
    if grid:
        @pl.when(outer)
        def _():
            for part in range(PARTS):
                send(0, None, RELAY, part, skip).start()
                send(2, None, 2, part, beside).start()
            for part in range(PARTS):
                send(1, None, 1, part, along).start()

        @pl.when(jnp.logical_not(outer))
        def _():
            for part in range(PARTS):
                send(0, None, 1, part, along).start()
                send(1, None, 2, part, beside).start()
    else:
        for part in range(PARTS):
            send(0, None, 1, part, along).start()
            send(1, None, 2, part, beside).start()
    for copy in first_copies:
        copy.start()

    def ring_poll(r):
        group, part = r // PARTS, r % PARTS
        arrived(1 + 2 * group, part)
        arrived(2 + 2 * group, part)

        @pl.when(group < SPAN - 1)
        def _():
            send(2 + 2 * group, 1 + 2 * group, 3 + 2 * group, part, along).start()
            send(3 + 2 * group, 2 + 2 * group, 4 + 2 * group, part, beside).start()

    def outer_poll(r):
        group, part = r // PARTS, r % PARTS
        arrived(1 + 2 * group, part)

        @pl.when(group < 2)
        def _():
            send(3 + group, 1 + 2 * group, 4 + 2 * group, part, beside).start()
        arrived(2 + 2 * group, part)

        @pl.when(group == 0)
        def _():
            send(5, 2, 3, part, along).start()

    def far_on(part):
        arrived(RELAY, part)
        send(3, RELAY, 3, part, along).start()
        send(4, RELAY, 4, part, beside).start()

    def corner_on(part):
        arrived(5, part)
        send(5, 5, 5, part, along).start()

    def inner_poll(r):
        if r < PARTS:
            arrived(2, r)
        if 1 <= r < 5:
            far_on(r - 1)
        if r == 2:
            for part in range(3):
                send(6, 2, 5, part, across).start()
        if r == 3:
            send(6, 2, 5, 3, across).start()
            for part in range(PARTS):
                send(2, None, 6, part, across).start()
        if 5 <= r < 9:
            corner_on(r - 5)
        if 4 <= r < 8:
            arrived(1, r - 4)
            arrived(4, r - 4)
        if 8 <= r < 12:
            arrived(3, r - 8)
        if 9 <= r:
            arrived(6, r - 9)

    inner_polls = {
        0: ((0,), (1, 2, 3)), 1: ((4,), (5,)), 2: ((6,), (7,)), 3: ((), (8,)), 4: ((9,), (10,)), 5: ((11,), (12,)),
    }

    def poll(j, second):
        ahead = j < steps
        if not grid:
            @pl.when(ahead)
            def _():
                ring_poll(2 * j + second)
            return

        @pl.when(jnp.logical_and(outer, ahead))
        def _():
            outer_poll(2 * j + second)

        @pl.when(jnp.logical_not(outer))
        def _():
            for at, polls in inner_polls.items():
                if polls[second]:
                    @pl.when(j == at)
                    def _(polls=polls):
                        for r in polls[second]:
                            inner_poll(r)

    peaks[...] = jnp.full(peaks.shape, LOW, jnp.float32)
    totals[...] = jnp.zeros(totals.shape, jnp.float32)
    acc[...] = jnp.zeros(acc.shape, jnp.float32)
    for load in loads[:4]:
        load.wait()

    def normed_of(raw):
        raw = raw.astype(jnp.float32)
        mean_sq = jnp.mean(raw * raw, axis=-1, keepdims=True)
        return (raw * lax.rsqrt(mean_sq + 1e-6) * in_gain[...]).astype(jnp.bfloat16)

    for copy in first_copies:
        copy.wait_recv()
    ids = jnp.zeros((8, 1), jnp.int32)
    line = lax.broadcasted_iota(jnp.int32, (8, 1), 0)
    for slot, at in enumerate(slot_chips(chip, chips)):
        ids = jnp.where(line == slot, at * 2 + core, ids)
    for side, query_view in enumerate((me, partner)):
        listed = lists[side]
        valid = lax.broadcasted_iota(jnp.int32, (8, listed.shape[1]), 1) < counts[side:side + 1, :]
        hits = jnp.where(((listed == ids) | (ids == query_view)) & valid, 1.0, 0.0)
        hit = jnp.max(hits, axis=1, keepdims=True)
        for slot in range(SLOTS):
            mask[slot, :, side * rows:(side + 1) * rows] = jnp.broadcast_to(hit[slot:slot + 1], (8, rows))

    loads[4].wait()
    query_in = jnp.concatenate([normed_of(buf[0]), normed_of(other[...])], axis=0)
    query = jnp.dot(query_in, wq[...], preferred_element_type=jnp.float32).astype(jnp.bfloat16)
    query = query.astype(jnp.float32) * HEAD_DIM ** (-0.5)
    query_t = query.T.astype(jnp.bfloat16)
    zero = jnp.zeros((HEAD_DIM, 2 * rows), jnp.bfloat16)
    for h in range(heads):
        mine = query_t[h * HEAD_DIM:(h + 1) * HEAD_DIM, :]
        qpad[h] = jnp.concatenate([mine, zero] if h % 2 == 0 else [zero, mine], axis=0)
    loads[5].wait()
    loads[6].wait()

    queries = 2 * rows
    tiles = rows // 16

    def project(first, second):
        normed = normed_of(jnp.concatenate([first, second], axis=0))
        key = jnp.dot(normed, wk[...], preferred_element_type=jnp.float32).astype(jnp.bfloat16)
        for pair in range(heads // 2):
            kbuf[pair] = key[:, pair * 2 * HEAD_DIM:(pair + 1) * 2 * HEAD_DIM]
        value = jnp.dot(normed, wv[...], preferred_element_type=jnp.float32)
        vtbuf[...] = value.T.astype(jnp.bfloat16).reshape(vtbuf.shape)

    def score(pair, at, scores):
        scores[at] = jnp.dot(kbuf[pair], qpad[2 * pair + at], preferred_element_type=jnp.float32)

    def weigh(pair, at, scores, weights, keep_ref, on_first, on_second):
        h = 2 * pair + at
        found = scores[at].reshape(2 * tiles, 8, queries)
        first, second = found[:tiles], found[tiles:]
        old = peaks[h]
        new = jnp.maximum(
            jnp.where(on_first, jnp.max(first, axis=0), -INF),
            jnp.where(on_second, jnp.max(second, axis=0), -INF),
        )
        new = jnp.maximum(old, jnp.broadcast_to(jnp.max(new, axis=0, keepdims=True), (8, queries)))
        e_first = jnp.exp(first - jnp.where(on_first, new, INF)[None])
        e_second = jnp.exp(second - jnp.where(on_second, new, INF)[None])
        keep = jnp.exp(old - new)
        peaks[h] = new
        keep_ref[at] = keep
        totals[h] = totals[h] * keep + (jnp.sum(e_first, axis=0) + jnp.sum(e_second, axis=0))
        weights[at] = jnp.concatenate([e_first, e_second], axis=0).reshape(rows, queries).astype(jnp.bfloat16)

    def gather(pair, at, weights, keep_ref):
        h = 2 * pair + at
        kept = acc[h].reshape(HEAD_DIM // 8, 8, queries) * keep_ref[at][None]
        acc[h] = kept.reshape(HEAD_DIM, queries) + jnp.dot(
            vtbuf[h], weights[at], preferred_element_type=jnp.float32
        )

    def attend(near, far, handed=None):
        on_first, on_second = mask[near] > 0.5, mask[far] > 0.5
        pairs = heads // 2
        sides = ((s_even, w_even, keeps.at[0]), (s_odd, w_odd, keeps.at[1]))

        def stage(pair, odd, ahead=True, behind=True):
            scores, weights, keep = sides[odd]
            next_scores, last_weights, last_keep = sides[1 - odd]
            for at in range(2):
                if ahead:
                    score(pair + 1, at, next_scores)
                if behind:
                    gather(pair - 1, at, last_weights, last_keep)
                weigh(pair, at, scores, weights, keep, on_first, on_second)

        for at in range(2):
            score(0, at, s_even)
        stage(0, 0, behind=False)
        if handed is None:
            def both(i, carry):
                stage(2 * i + 1, 1)
                stage(2 * i + 2, 0)
                return carry

            lax.fori_loop(0, pairs // 2 - 1, both, 0)
        else:
            for pair in range(1, pairs - 1):
                stage(pair, pair % 2)
                if (pair * 2) % GROUP == 0:
                    handed(pair * 2 // GROUP - 1)
        stage(pairs - 1, 1, ahead=False)
        for at in range(2):
            gather(pairs - 1, at, w_odd, keeps.at[1])
        if handed is not None:
            handed(groups - 1)

    def pick(table, j):
        found = table[0]
        for at in range(1, len(table)):
            found = jnp.where(j == at, table[at], found)
        return found

    def step(j, carry):
        if grid:
            picks = [
                jnp.where(outer, pick(far, j), pick(near, j))
                for far, near in zip(zip(*OUTER_STEPS), zip(*INNER_STEPS))
            ]
        else:
            picks = [pick(column, j) for column in zip(*OUTER_STEPS)]
        near, near_half, far, far_half = picks
        near_row = pl.multiple_of(near_half * half, half)
        far_row = pl.multiple_of(far_half * half, half)
        project(buf[near, pl.ds(near_row, half)], buf[far, pl.ds(far_row, half)])
        poll(j, 0)
        attend(near, far)
        poll(j, 1)
        return carry

    lax.fori_loop(0, steps, step, 0)

    def stats_swap(group):
        return partner_copy(stats_out.at[group], stats_in.at[group], 3 + group)

    def acc_swap(group):
        members = pl.ds(group * GROUP, GROUP)
        return partner_copy(acc.at[members, :, pl.ds(rows, rows)], acc_in.at[members], 3 + groups + group)

    def totals_of(h, side):
        return jnp.sum(totals[h][:, side * rows:(side + 1) * rows], axis=0, keepdims=True)

    def hand(group):
        acc_swap(group).start()
        members = range(group * GROUP, (group + 1) * GROUP)
        stats_out[group] = jnp.concatenate(
            [peaks[h][:1, rows:] for h in members] + [totals_of(h, 1) for h in members], axis=0
        )
        stats_swap(group).start()

    if grid:
        near, far = (jnp.where(outer, OUTER_STEPS[-1][at], INNER_STEPS[-1][at]) for at in (0, 2))
    else:
        near, far = (jnp.int32(OUTER_STEPS[-1][at]) for at in (0, 2))
    span = pl.ds(half, half)
    project(buf[near, span], buf[far, span])
    attend(near, far, hand)

    for part in range(PARTS):
        for kind in range(6):
            send(kind, None, 1, part, partner).wait_send()
        if grid:
            @pl.when(jnp.logical_not(outer))
            def _(part=part):
                send(6, None, 1, part, partner).wait_send()
    for copy in first_copies:
        copy.wait_send()
    loads[7].wait()
    loads[8].wait()
    update = buf[0].astype(jnp.float32)
    for group in range(groups):
        stats_swap(group).wait_recv()
        acc_swap(group).wait_recv()
        pieces = []
        for at, h in enumerate(range(group * GROUP, (group + 1) * GROUP)):
            peak, peak_in = peaks[h][:1, :rows], stats_in[group, at:at + 1, :]
            new = jnp.maximum(peak, peak_in)
            keep, keep_in = jnp.exp(peak - new), jnp.exp(peak_in - new)
            total = totals_of(h, 0) * keep + stats_in[group, GROUP + at:GROUP + at + 1, :] * keep_in
            attended = (acc[h, :, :rows] * keep + acc_in[h] * keep_in) / total
            mean_sq = jnp.mean(attended * attended, axis=0, keepdims=True)
            pieces.append(attended * lax.rsqrt(mean_sq + 1e-6))
        feats = slice(group * GROUP * HEAD_DIM, (group + 1) * GROUP * HEAD_DIM)
        head_normed = (jnp.concatenate(pieces, axis=0).T * out_gain[:, feats]).astype(jnp.bfloat16)
        update = update + jnp.dot(head_normed, wo[feats, :], preferred_element_type=jnp.float32)
    out_ref[...] = update.astype(out_ref.dtype)

    for group in range(groups):
        stats_swap(group).wait_send()
        acc_swap(group).wait_send()


def on_device(tokens, in_gain, w_query, w_key, w_value, w_out, out_gain, covis_list, covis_count):
    views = lax.axis_size("views")
    rows, width = tokens.shape[1:]
    slots_listed = covis_list.shape[1]
    hbm = pl.BlockSpec(memory_space=pltpu.HBM)
    vmem = pl.BlockSpec(memory_space=pltpu.VMEM)
    bf16, f32 = jnp.bfloat16, jnp.float32
    heads = width // HEAD_DIM
    dma = pltpu.SemaphoreType.DMA
    out = pl.pallas_call(
        functools.partial(body, views),
        out_shape=jax.ShapeDtypeStruct((rows, width), tokens.dtype),
        in_specs=[hbm] * 9,
        out_specs=vmem,
        scratch_shapes=[
            pltpu.VMEM((SLOTS, rows, width), bf16),
            pltpu.VMEM((rows, width), bf16),
            pltpu.VMEM((width, width), bf16),
            pltpu.VMEM((width, width), bf16),
            pltpu.VMEM((width, width), bf16),
            pltpu.VMEM((width, width), bf16),
            pltpu.VMEM((1, width), f32),
            pltpu.VMEM((1, width), f32),
            pltpu.VMEM((2, 1, slots_listed), jnp.int32),
            pltpu.VMEM((2, 1), jnp.int32),
            pltpu.VMEM((heads, 2 * HEAD_DIM, 2 * rows), bf16),
            pltpu.VMEM((heads // 2, rows, 2 * HEAD_DIM), bf16),
            pltpu.VMEM((heads, HEAD_DIM, rows), bf16),
            pltpu.VMEM((heads, 8, 2 * rows), f32),
            pltpu.VMEM((heads, 8, 2 * rows), f32),
            pltpu.VMEM((heads, HEAD_DIM, 2 * rows), f32),
            pltpu.VMEM((SLOTS, 8, 2 * rows), f32),
            pltpu.VMEM((heads // GROUP, 2 * GROUP, rows), f32),
            pltpu.VMEM((heads // GROUP, 2 * GROUP, rows), f32),
            pltpu.VMEM((heads, HEAD_DIM, rows), f32),
            pltpu.VMEM((2, rows, 2 * rows), f32),
            pltpu.VMEM((2, rows, 2 * rows), f32),
            pltpu.VMEM((2, rows, 2 * rows), bf16),
            pltpu.VMEM((2, rows, 2 * rows), bf16),
            pltpu.VMEM((2, 2, 8, 2 * rows), f32),
            dma((9,)),
            dma((8, PARTS)),
            dma((SLOTS, PARTS)),
            dma((3 + 2 * (heads // GROUP),)),
            dma((3 + 2 * (heads // GROUP),)),
        ],
        compiler_params=pltpu.CompilerParams(
            collective_id=0, has_side_effects=True, vmem_limit_bytes=32 * 1024 * 1024
        ),
    )(*(pltpu.with_memory_space_constraint(a, pltpu.HBM) for a in (tokens[0], in_gain[None], w_query, w_key, w_value, w_out, out_gain[None], covis_list)), covis_count)
    return out[None]


def solution(mesh):
    in_specs = (
        P(("groups", "views"), None, None),
        P(), P(), P(), P(), P(), P(),
        P(("groups", "views"), None),
        P(("groups", "views")),
    )
    out_specs = P(("groups", "views"), None, None)
    return jax.shard_map(on_device, mesh=mesh, in_specs=in_specs, out_specs=out_specs, check_vma=False)
```

```python
import functools

import jax
import jax.numpy as jnp
from jax import lax
from jax.experimental import pallas as pl
from jax.experimental.pallas import tpu as pltpu
from jax.sharding import PartitionSpec as P

HEADS = 16
HEAD_DIM = 64
REACH = 6
SPAN = REACH // 2
SLOTS = 2 * SPAN + 2
RELAY = SLOTS - 1
PARTS = 4
ROUNDS = SPAN * PARTS
GROUP = 4
MESH = pl.DeviceIdType.MESH
INF = float("inf")
LOW = -3e38


def is_grid(chips):
    return chips == 2 * SPAN + 2


def grid_chip(chip, mirror, depth, side):
    z, y = chip // 2, chip % 2
    if depth:
        z = z + 1 - 2 * (z % 2)
    if mirror:
        z = 3 - z
    if side:
        y = 1 - y
    return 2 * z + y


OUTER_SLOTS = ((0, 0, 0), (0, 1, 0), (0, 0, 1), (1, 0, 0), (0, 1, 1), (1, 1, 1), (1, 0, 1))
INNER_SLOTS = ((0, 0, 0), (0, 1, 0), (0, 0, 1), (0, 1, 1), (1, 1, 1), (1, 0, 1), (1, 0, 0))
INNER_STEPS = ((0, 0, 0, 1), (2, 0, 2, 1), (1, 0, 4, 0), (1, 1, 4, 1), (5, 0, 5, 1), (3, 0, 6, 0), (3, 1, 6, 1))
OUTER_STEPS = ((0, 0, 0, 1),) + tuple(
    (1 + 2 * group, late, 2 + 2 * group, late) for group in range(SPAN) for late in range(2)
)


def slot_chips(chip, chips):
    if is_grid(chips):
        outer = (chip // 2) % 3 == 0
        return [
            jnp.where(outer, grid_chip(chip, *far), grid_chip(chip, *near))
            for far, near in zip(OUTER_SLOTS, INNER_SLOTS)
        ]
    found = [chip]
    for hops in range(1, SPAN + 1):
        found += [(chip - hops + chips) % chips, (chip + hops) % chips]
    return found


def body(
    views, tok_hbm, in_gain_hbm, wq_hbm, wk_hbm, wv_hbm, wo_hbm, out_gain_hbm, list_hbm, count_hbm,
    out_ref,
    buf, other, wq, wk, wv, wo, in_gain, out_gain, lists, counts, qpad, kbuf, vtbuf,
    peaks, totals, acc, mask, stats_out, stats_in, acc_in,
    s_even, s_odd, w_even, w_odd, keeps,
    load_sem, send_sem, recv_sem, misc_send, misc_recv,
):
    chips = views // 2
    grid = is_grid(chips)
    me = lax.axis_index("views")
    chip, core = me // 2, me % 2
    partner = chip * 2 + 1 - core
    rows, width = tok_hbm.shape
    heads = width // HEAD_DIM
    size = rows // PARTS
    half = rows // 2
    steps = ROUNDS // 2
    groups = heads // GROUP

    loads = [
        pltpu.make_async_copy(tok_hbm, buf.at[0], load_sem.at[0]),
        pltpu.make_async_copy(in_gain_hbm, in_gain, load_sem.at[5]),
        pltpu.make_async_copy(list_hbm, lists.at[0], load_sem.at[7]),
        pltpu.make_async_copy(count_hbm, counts.at[0], load_sem.at[8]),
        pltpu.make_async_copy(wq_hbm, wq, load_sem.at[1]),
        pltpu.make_async_copy(wk_hbm, wk, load_sem.at[2]),
        pltpu.make_async_copy(wv_hbm, wv, load_sem.at[3]),
        pltpu.make_async_copy(out_gain_hbm, out_gain, load_sem.at[6]),
        pltpu.make_async_copy(wo_hbm, wo, load_sem.at[4]),
    ]

    if grid:
        outer = (chip // 2) % 3 == 0
        beside = grid_chip(chip, 0, 0, 1) * 2 + core
        along = grid_chip(chip, 0, 1, 0) * 2 + core
        across = grid_chip(chip, 1, 0, 0) * 2 + core
        skip = grid_chip(chip, 1, 1, 0) * 2 + core
    else:
        outer = None
        beside = (chip + chips - 1) % chips * 2 + core
        along = (chip + 1) % chips * 2 + core

    barrier = pltpu.get_barrier_semaphore()
    for device in (partner, beside, along):
        pl.semaphore_signal(barrier, inc=1, device_id={"views": device}, device_id_type=MESH)
    if grid:
        @pl.when(jnp.logical_not(outer))
        def _():
            for device in (across, skip):
                pl.semaphore_signal(barrier, inc=1, device_id={"views": device}, device_id_type=MESH)
    for load in loads:
        load.start()
    pl.semaphore_wait(barrier, 4 if grid else 3)

    def send(kind, source, slot, part, device):
        span = pl.ds(pl.multiple_of(part * size, size), size)
        return pltpu.make_async_remote_copy(
            src_ref=tok_hbm.at[span] if source is None else buf.at[source, span],
            dst_ref=buf.at[slot, span],
            send_sem=send_sem.at[kind, part],
            recv_sem=recv_sem.at[slot, part],
            device_id={"views": device},
            device_id_type=MESH,
        )

    def arrived(slot, part):
        send(0, slot, slot, part, partner).wait_recv()

    def partner_copy(src, dst, index):
        return pltpu.make_async_remote_copy(
            src_ref=src, dst_ref=dst, send_sem=misc_send.at[index], recv_sem=misc_recv.at[index],
            device_id={"views": partner}, device_id_type=MESH,
        )

    first_copies = [
        partner_copy(tok_hbm, other, 0),
        partner_copy(list_hbm, lists.at[1], 1),
        partner_copy(count_hbm, counts.at[1], 2),
    ]
    if grid:
        @pl.when(outer)
        def _():
            for part in range(PARTS):
                send(0, None, RELAY, part, skip).start()
                send(2, None, 2, part, beside).start()
            for part in range(PARTS):
                send(1, None, 1, part, along).start()

        @pl.when(jnp.logical_not(outer))
        def _():
            for part in range(PARTS):
                send(0, None, 1, part, along).start()
                send(1, None, 2, part, beside).start()
    else:
        for part in range(PARTS):
            send(0, None, 1, part, along).start()
            send(1, None, 2, part, beside).start()
    for copy in first_copies:
        copy.start()

    def ring_poll(r):
        group, part = r // PARTS, r % PARTS
        arrived(1 + 2 * group, part)
        arrived(2 + 2 * group, part)

        @pl.when(group < SPAN - 1)
        def _():
            send(2 + 2 * group, 1 + 2 * group, 3 + 2 * group, part, along).start()
            send(3 + 2 * group, 2 + 2 * group, 4 + 2 * group, part, beside).start()

    def outer_poll(r):
        group, part = r // PARTS, r % PARTS
        arrived(1 + 2 * group, part)

        @pl.when(group < 2)
        def _():
            send(3 + group, 1 + 2 * group, 4 + 2 * group, part, beside).start()
        arrived(2 + 2 * group, part)

        @pl.when(group == 0)
        def _():
            send(5, 2, 3, part, along).start()

    def far_on(part):
        arrived(RELAY, part)
        send(3, RELAY, 3, part, along).start()
        send(4, RELAY, 4, part, beside).start()

    def corner_on(part):
        arrived(5, part)
        send(5, 5, 5, part, along).start()

    def inner_poll(r):
        if r < PARTS:
            arrived(2, r)
        if 1 <= r < 5:
            far_on(r - 1)
        if r == 2:
            for part in range(3):
                send(6, 2, 5, part, across).start()
        if r == 3:
            send(6, 2, 5, 3, across).start()
            for part in range(PARTS):
                send(2, None, 6, part, across).start()
        if 5 <= r < 9:
            corner_on(r - 5)
        if 4 <= r < 8:
            arrived(1, r - 4)
            arrived(4, r - 4)
        if 8 <= r < 12:
            arrived(3, r - 8)
        if 9 <= r:
            arrived(6, r - 9)

    inner_polls = {
        0: ((0,), (1, 2, 3)), 1: ((4,), (5,)), 2: ((6,), (7,)), 3: ((), (8,)), 4: ((9,), (10,)), 5: ((11,), (12,)),
    }

    def poll(j, second):
        ahead = j < steps
        if not grid:
            @pl.when(ahead)
            def _():
                ring_poll(2 * j + second)
            return

        @pl.when(jnp.logical_and(outer, ahead))
        def _():
            outer_poll(2 * j + second)

        @pl.when(jnp.logical_not(outer))
        def _():
            for at, polls in inner_polls.items():
                if polls[second]:
                    @pl.when(j == at)
                    def _(polls=polls):
                        for r in polls[second]:
                            inner_poll(r)

    peaks[...] = jnp.full(peaks.shape, LOW, jnp.float32)
    totals[...] = jnp.zeros(totals.shape, jnp.float32)
    acc[...] = jnp.zeros(acc.shape, jnp.float32)
    for load in loads[:4]:
        load.wait()

    def normed_of(raw):
        raw = raw.astype(jnp.float32)
        mean_sq = jnp.mean(raw * raw, axis=-1, keepdims=True)
        return (raw * lax.rsqrt(mean_sq + 1e-6) * in_gain[...]).astype(jnp.bfloat16)

    for copy in first_copies:
        copy.wait_recv()
    ids = jnp.zeros((8, 1), jnp.int32)
    line = lax.broadcasted_iota(jnp.int32, (8, 1), 0)
    for slot, at in enumerate(slot_chips(chip, chips)):
        ids = jnp.where(line == slot, at * 2 + core, ids)
    for side, query_view in enumerate((me, partner)):
        listed = lists[side]
        valid = lax.broadcasted_iota(jnp.int32, (8, listed.shape[1]), 1) < counts[side:side + 1, :]
        hits = jnp.where(((listed == ids) | (ids == query_view)) & valid, 1.0, 0.0)
        hit = jnp.max(hits, axis=1, keepdims=True)
        for slot in range(SLOTS):
            mask[slot, :, side * rows:(side + 1) * rows] = jnp.broadcast_to(hit[slot:slot + 1], (8, rows))

    loads[4].wait()
    query_in = jnp.concatenate([normed_of(buf[0]), normed_of(other[...])], axis=0)
    query = jnp.dot(query_in, wq[...], preferred_element_type=jnp.float32).astype(jnp.bfloat16)
    query = query.astype(jnp.float32) * HEAD_DIM ** (-0.5)
    query_t = query.T.astype(jnp.bfloat16)
    zero = jnp.zeros((HEAD_DIM, 2 * rows), jnp.bfloat16)
    for h in range(heads):
        mine = query_t[h * HEAD_DIM:(h + 1) * HEAD_DIM, :]
        qpad[h] = jnp.concatenate([mine, zero] if h % 2 == 0 else [zero, mine], axis=0)
    loads[5].wait()
    loads[6].wait()

    queries = 2 * rows
    tiles = rows // 16

    def project(first, second):
        normed = normed_of(jnp.concatenate([first, second], axis=0))
        key = jnp.dot(normed, wk[...], preferred_element_type=jnp.float32).astype(jnp.bfloat16)
        for pair in range(heads // 2):
            kbuf[pair] = key[:, pair * 2 * HEAD_DIM:(pair + 1) * 2 * HEAD_DIM]
        value = jnp.dot(normed, wv[...], preferred_element_type=jnp.float32)
        vtbuf[...] = value.T.astype(jnp.bfloat16).reshape(vtbuf.shape)

    def score(pair, at, scores):
        scores[at] = jnp.dot(kbuf[pair], qpad[2 * pair + at % 2], preferred_element_type=jnp.float32)

    def weigh(pair, at, scores, weights, keep_ref, on_first, on_second):
        h = 2 * pair + at % 2
        found = scores[at].reshape(2 * tiles, 8, queries)
        first, second = found[:tiles], found[tiles:]
        old = peaks[h]
        new = jnp.maximum(
            jnp.where(on_first, jnp.max(first, axis=0), -INF),
            jnp.where(on_second, jnp.max(second, axis=0), -INF),
        )
        new = jnp.maximum(old, jnp.broadcast_to(jnp.max(new, axis=0, keepdims=True), (8, queries)))
        e_first = jnp.exp(first - jnp.where(on_first, new, INF)[None])
        e_second = jnp.exp(second - jnp.where(on_second, new, INF)[None])
        keep = jnp.exp(old - new)
        peaks[h] = new
        keep_ref[at] = keep
        totals[h] = totals[h] * keep + (jnp.sum(e_first, axis=0) + jnp.sum(e_second, axis=0))
        weights[at] = jnp.concatenate([e_first, e_second], axis=0).reshape(rows, queries).astype(jnp.bfloat16)

    def gather(pair, at, weights, keep_ref):
        h = 2 * pair + at % 2
        kept = acc[h].reshape(HEAD_DIM // 8, 8, queries) * keep_ref[at][None]
        acc[h] = kept.reshape(HEAD_DIM, queries) + jnp.dot(
            vtbuf[h], weights[at], preferred_element_type=jnp.float32
        )

    def attend(near, far, handed=None):
        on_first, on_second = mask[near] > 0.5, mask[far] > 0.5
        sides = ((s_even, w_even, keeps.at[0]), (s_odd, w_odd, keeps.at[1]))

        def score_all(group, scores):
            for at in range(GROUP):
                score((GROUP // 2) * group + at // 2, at, scores)

        def gather_all(group, weights, keep):
            for at in range(GROUP):
                gather((GROUP // 2) * group + at // 2, at, weights, keep)

        def stage(group, odd, ahead=True, behind=True):
            scores, weights, keep = sides[odd]
            next_scores, last_weights, last_keep = sides[1 - odd]
            if ahead:
                score_all(group + 1, next_scores)
            if behind:
                gather_all(group - 1, last_weights, last_keep)
            for at in range(GROUP):
                weigh((GROUP // 2) * group + at // 2, at, scores, weights, keep, on_first, on_second)

        score_all(0, s_even)
        stage(0, 0, behind=False)
        if handed is None:
            for group in range(1, groups - 1):
                stage(group, group % 2)
        else:
            for group in range(1, groups - 1):
                stage(group, group % 2)
                handed(group - 1)
        stage(groups - 1, 1, ahead=False)
        if handed is not None:
            handed(groups - 2)
        gather_all(groups - 1, w_odd, keeps.at[1])
        if handed is not None:
            handed(groups - 1)

    def pick(table, j):
        found = table[0]
        for at in range(1, len(table)):
            found = jnp.where(j == at, table[at], found)
        return found

    def step(j, carry):
        if grid:
            picks = [
                jnp.where(outer, pick(far, j), pick(near, j))
                for far, near in zip(zip(*OUTER_STEPS), zip(*INNER_STEPS))
            ]
        else:
            picks = [pick(column, j) for column in zip(*OUTER_STEPS)]
        near, near_half, far, far_half = picks
        near_row = pl.multiple_of(near_half * half, half)
        far_row = pl.multiple_of(far_half * half, half)
        project(buf[near, pl.ds(near_row, half)], buf[far, pl.ds(far_row, half)])
        poll(j, 0)
        attend(near, far)
        poll(j, 1)
        return carry

    lax.fori_loop(0, steps, step, 0)

    def stats_swap(group):
        return partner_copy(stats_out.at[group], stats_in.at[group], 3 + group)

    def acc_swap(group):
        members = pl.ds(group * GROUP, GROUP)
        return partner_copy(acc.at[members, :, pl.ds(rows, rows)], acc_in.at[members], 3 + groups + group)

    def totals_of(h, side):
        return jnp.sum(totals[h][:, side * rows:(side + 1) * rows], axis=0, keepdims=True)

    def hand(group):
        acc_swap(group).start()
        members = range(group * GROUP, (group + 1) * GROUP)
        stats_out[group] = jnp.concatenate(
            [peaks[h][:1, rows:] for h in members] + [totals_of(h, 1) for h in members], axis=0
        )
        stats_swap(group).start()

    if grid:
        near, far = (jnp.where(outer, OUTER_STEPS[-1][at], INNER_STEPS[-1][at]) for at in (0, 2))
    else:
        near, far = (jnp.int32(OUTER_STEPS[-1][at]) for at in (0, 2))
    span = pl.ds(half, half)
    project(buf[near, span], buf[far, span])
    attend(near, far, hand)

    for part in range(PARTS):
        for kind in range(6):
            send(kind, None, 1, part, partner).wait_send()
        if grid:
            @pl.when(jnp.logical_not(outer))
            def _(part=part):
                send(6, None, 1, part, partner).wait_send()
    for copy in first_copies:
        copy.wait_send()
    loads[7].wait()
    loads[8].wait()
    update = buf[0].astype(jnp.float32)
    for group in range(groups):
        stats_swap(group).wait_recv()
        acc_swap(group).wait_recv()
        pieces = []
        for at, h in enumerate(range(group * GROUP, (group + 1) * GROUP)):
            peak, peak_in = peaks[h][:1, :rows], stats_in[group, at:at + 1, :]
            new = jnp.maximum(peak, peak_in)
            keep, keep_in = jnp.exp(peak - new), jnp.exp(peak_in - new)
            total = totals_of(h, 0) * keep + stats_in[group, GROUP + at:GROUP + at + 1, :] * keep_in
            attended = (acc[h, :, :rows] * keep + acc_in[h] * keep_in) / total
            mean_sq = jnp.mean(attended * attended, axis=0, keepdims=True)
            pieces.append(attended * lax.rsqrt(mean_sq + 1e-6))
        feats = slice(group * GROUP * HEAD_DIM, (group + 1) * GROUP * HEAD_DIM)
        head_normed = (jnp.concatenate(pieces, axis=0).T * out_gain[:, feats]).astype(jnp.bfloat16)
        update = update + jnp.dot(head_normed, wo[feats, :], preferred_element_type=jnp.float32)
    out_ref[...] = update.astype(out_ref.dtype)

    for group in range(groups):
        stats_swap(group).wait_send()
        acc_swap(group).wait_send()


def on_device(tokens, in_gain, w_query, w_key, w_value, w_out, out_gain, covis_list, covis_count):
    views = lax.axis_size("views")
    rows, width = tokens.shape[1:]
    slots_listed = covis_list.shape[1]
    hbm = pl.BlockSpec(memory_space=pltpu.HBM)
    vmem = pl.BlockSpec(memory_space=pltpu.VMEM)
    bf16, f32 = jnp.bfloat16, jnp.float32
    heads = width // HEAD_DIM
    dma = pltpu.SemaphoreType.DMA
    out = pl.pallas_call(
        functools.partial(body, views),
        out_shape=jax.ShapeDtypeStruct((rows, width), tokens.dtype),
        in_specs=[hbm] * 9,
        out_specs=vmem,
        scratch_shapes=[
            pltpu.VMEM((SLOTS, rows, width), bf16),
            pltpu.VMEM((rows, width), bf16),
            pltpu.VMEM((width, width), bf16),
            pltpu.VMEM((width, width), bf16),
            pltpu.VMEM((width, width), bf16),
            pltpu.VMEM((width, width), bf16),
            pltpu.VMEM((1, width), f32),
            pltpu.VMEM((1, width), f32),
            pltpu.VMEM((2, 1, slots_listed), jnp.int32),
            pltpu.VMEM((2, 1), jnp.int32),
            pltpu.VMEM((heads, 2 * HEAD_DIM, 2 * rows), bf16),
            pltpu.VMEM((heads // 2, rows, 2 * HEAD_DIM), bf16),
            pltpu.VMEM((heads, HEAD_DIM, rows), bf16),
            pltpu.VMEM((heads, 8, 2 * rows), f32),
            pltpu.VMEM((heads, 8, 2 * rows), f32),
            pltpu.VMEM((heads, HEAD_DIM, 2 * rows), f32),
            pltpu.VMEM((SLOTS, 8, 2 * rows), f32),
            pltpu.VMEM((heads // GROUP, 2 * GROUP, rows), f32),
            pltpu.VMEM((heads // GROUP, 2 * GROUP, rows), f32),
            pltpu.VMEM((heads, HEAD_DIM, rows), f32),
            pltpu.VMEM((GROUP, rows, 2 * rows), f32),
            pltpu.VMEM((GROUP, rows, 2 * rows), f32),
            pltpu.VMEM((GROUP, rows, 2 * rows), bf16),
            pltpu.VMEM((GROUP, rows, 2 * rows), bf16),
            pltpu.VMEM((2, GROUP, 8, 2 * rows), f32),
            dma((9,)),
            dma((8, PARTS)),
            dma((SLOTS, PARTS)),
            dma((3 + 2 * (heads // GROUP),)),
            dma((3 + 2 * (heads // GROUP),)),
        ],
        compiler_params=pltpu.CompilerParams(
            collective_id=0, has_side_effects=True, vmem_limit_bytes=32 * 1024 * 1024
        ),
    )(*(pltpu.with_memory_space_constraint(a, pltpu.HBM) for a in (tokens[0], in_gain[None], w_query, w_key, w_value, w_out, out_gain[None], covis_list)), covis_count)
    return out[None]


def solution(mesh):
    in_specs = (
        P(("groups", "views"), None, None),
        P(), P(), P(), P(), P(), P(),
        P(("groups", "views"), None),
        P(("groups", "views")),
    )
    out_specs = P(("groups", "views"), None, None)
    return jax.shard_map(on_device, mesh=mesh, in_specs=in_specs, out_specs=out_specs, check_vma=False)
```

```python
import functools

import jax
import jax.numpy as jnp
from jax import lax
from jax.experimental import pallas as pl
from jax.experimental.pallas import tpu as pltpu
from jax.sharding import PartitionSpec as P

HEADS = 16
HEAD_DIM = 64
REACH = 6
SPAN = REACH // 2
SLOTS = 2 * SPAN + 2
RELAY = SLOTS - 1
PARTS = 4
ROUNDS = SPAN * PARTS
GROUP = 4
MESH = pl.DeviceIdType.MESH
INF = float("inf")
LOW = -3e38


def is_grid(chips):
    return chips == 2 * SPAN + 2


def grid_chip(chip, mirror, depth, side):
    z, y = chip // 2, chip % 2
    if depth:
        z = z + 1 - 2 * (z % 2)
    if mirror:
        z = 3 - z
    if side:
        y = 1 - y
    return 2 * z + y


OUTER_SLOTS = ((0, 0, 0), (0, 1, 0), (0, 0, 1), (1, 0, 0), (0, 1, 1), (1, 1, 1), (1, 0, 1))
INNER_SLOTS = ((0, 0, 0), (0, 1, 0), (0, 0, 1), (0, 1, 1), (1, 1, 1), (1, 0, 1), (1, 0, 0))
INNER_STEPS = ((0, 0, 0, 1), (2, 0, 2, 1), (1, 0, 4, 0), (1, 1, 4, 1), (5, 0, 5, 1), (3, 0, 6, 0), (3, 1, 6, 1))
OUTER_STEPS = ((0, 0, 0, 1),) + tuple(
    (1 + 2 * group, late, 2 + 2 * group, late) for group in range(SPAN) for late in range(2)
)


def slot_chips(chip, chips):
    if is_grid(chips):
        outer = (chip // 2) % 3 == 0
        return [
            jnp.where(outer, grid_chip(chip, *far), grid_chip(chip, *near))
            for far, near in zip(OUTER_SLOTS, INNER_SLOTS)
        ]
    found = [chip]
    for hops in range(1, SPAN + 1):
        found += [(chip - hops + chips) % chips, (chip + hops) % chips]
    return found


def body(
    views, tok_hbm, in_gain_hbm, wq_hbm, wk_hbm, wv_hbm, wo_hbm, out_gain_hbm, list_hbm, count_hbm,
    out_ref,
    buf, other, wq, wk, wv, wo, in_gain, out_gain, lists, counts, qpad, kbuf, vtbuf,
    peaks, totals, acc, mask, stats_out, stats_in, acc_in,
    s_even, s_odd, w_even, w_odd, keeps,
    load_sem, send_sem, recv_sem, misc_send, misc_recv,
):
    chips = views // 2
    grid = is_grid(chips)
    me = lax.axis_index("views")
    chip, core = me // 2, me % 2
    partner = chip * 2 + 1 - core
    rows, width = tok_hbm.shape
    heads = width // HEAD_DIM
    size = rows // PARTS
    half = rows // 2
    steps = ROUNDS // 2
    groups = heads // GROUP

    loads = [
        pltpu.make_async_copy(tok_hbm, buf.at[0], load_sem.at[0]),
        pltpu.make_async_copy(in_gain_hbm, in_gain, load_sem.at[5]),
        pltpu.make_async_copy(list_hbm, lists.at[0], load_sem.at[7]),
        pltpu.make_async_copy(count_hbm, counts.at[0], load_sem.at[8]),
        pltpu.make_async_copy(wq_hbm, wq, load_sem.at[1]),
        pltpu.make_async_copy(wk_hbm, wk, load_sem.at[2]),
        pltpu.make_async_copy(wv_hbm, wv, load_sem.at[3]),
        pltpu.make_async_copy(out_gain_hbm, out_gain, load_sem.at[6]),
        pltpu.make_async_copy(wo_hbm, wo, load_sem.at[4]),
    ]

    if grid:
        outer = (chip // 2) % 3 == 0
        beside = grid_chip(chip, 0, 0, 1) * 2 + core
        along = grid_chip(chip, 0, 1, 0) * 2 + core
        across = grid_chip(chip, 1, 0, 0) * 2 + core
        skip = grid_chip(chip, 1, 1, 0) * 2 + core
    else:
        outer = None
        beside = (chip + chips - 1) % chips * 2 + core
        along = (chip + 1) % chips * 2 + core

    barrier = pltpu.get_barrier_semaphore()
    for device in (partner, beside, along):
        pl.semaphore_signal(barrier, inc=1, device_id={"views": device}, device_id_type=MESH)
    if grid:
        @pl.when(jnp.logical_not(outer))
        def _():
            for device in (across, skip):
                pl.semaphore_signal(barrier, inc=1, device_id={"views": device}, device_id_type=MESH)
    for load in loads:
        load.start()
    pl.semaphore_wait(barrier, 4 if grid else 3)

    def send(kind, source, slot, part, device):
        span = pl.ds(pl.multiple_of(part * size, size), size)
        return pltpu.make_async_remote_copy(
            src_ref=tok_hbm.at[span] if source is None else buf.at[source, span],
            dst_ref=buf.at[slot, span],
            send_sem=send_sem.at[kind, part],
            recv_sem=recv_sem.at[slot, part],
            device_id={"views": device},
            device_id_type=MESH,
        )

    def arrived(slot, part):
        send(0, slot, slot, part, partner).wait_recv()

    def partner_copy(src, dst, index):
        return pltpu.make_async_remote_copy(
            src_ref=src, dst_ref=dst, send_sem=misc_send.at[index], recv_sem=misc_recv.at[index],
            device_id={"views": partner}, device_id_type=MESH,
        )

    first_copies = [
        partner_copy(tok_hbm, other, 0),
        partner_copy(list_hbm, lists.at[1], 1),
        partner_copy(count_hbm, counts.at[1], 2),
    ]
    if grid:
        @pl.when(outer)
        def _():
            for part in range(PARTS):
                send(0, None, RELAY, part, skip).start()
                send(2, None, 2, part, beside).start()
            for part in range(PARTS):
                send(1, None, 1, part, along).start()

        @pl.when(jnp.logical_not(outer))
        def _():
            for part in range(PARTS):
                send(0, None, 1, part, along).start()
                send(1, None, 2, part, beside).start()
    else:
        for part in range(PARTS):
            send(0, None, 1, part, along).start()
            send(1, None, 2, part, beside).start()
    for copy in first_copies:
        copy.start()

    def ring_poll(r):
        group, part = r // PARTS, r % PARTS
        arrived(1 + 2 * group, part)
        arrived(2 + 2 * group, part)

        @pl.when(group < SPAN - 1)
        def _():
            send(2 + 2 * group, 1 + 2 * group, 3 + 2 * group, part, along).start()
            send(3 + 2 * group, 2 + 2 * group, 4 + 2 * group, part, beside).start()

    def outer_poll(r):
        group, part = r // PARTS, r % PARTS
        arrived(1 + 2 * group, part)

        @pl.when(group < 2)
        def _():
            send(3 + group, 1 + 2 * group, 4 + 2 * group, part, beside).start()
        arrived(2 + 2 * group, part)

        @pl.when(group == 0)
        def _():
            send(5, 2, 3, part, along).start()

    def far_on(part):
        arrived(RELAY, part)
        send(3, RELAY, 3, part, along).start()
        send(4, RELAY, 4, part, beside).start()

    def corner_on(part):
        arrived(5, part)
        send(5, 5, 5, part, along).start()

    def inner_poll(r):
        if r < PARTS:
            arrived(2, r)
        if 1 <= r < 5:
            far_on(r - 1)
        if r == 2:
            for part in range(3):
                send(6, 2, 5, part, across).start()
        if r == 3:
            send(6, 2, 5, 3, across).start()
            for part in range(PARTS):
                send(2, None, 6, part, across).start()
        if 5 <= r < 9:
            corner_on(r - 5)
        if 4 <= r < 8:
            arrived(1, r - 4)
            arrived(4, r - 4)
        if 8 <= r < 12:
            arrived(3, r - 8)
        if 9 <= r:
            arrived(6, r - 9)

    inner_polls = {
        0: ((0,), (1, 2, 3)), 1: ((4,), (5,)), 2: ((6,), (7,)), 3: ((), (8,)), 4: ((9,), (10,)), 5: ((11,), (12,)),
    }

    def poll(j, second):
        ahead = j < steps
        if not grid:
            @pl.when(ahead)
            def _():
                ring_poll(2 * j + second)
            return

        @pl.when(jnp.logical_and(outer, ahead))
        def _():
            outer_poll(2 * j + second)

        @pl.when(jnp.logical_not(outer))
        def _():
            for at, polls in inner_polls.items():
                if polls[second]:
                    @pl.when(j == at)
                    def _(polls=polls):
                        for r in polls[second]:
                            inner_poll(r)

    peaks[...] = jnp.full(peaks.shape, LOW, jnp.float32)
    totals[...] = jnp.zeros(totals.shape, jnp.float32)
    acc[...] = jnp.zeros(acc.shape, jnp.float32)
    for load in loads[:4]:
        load.wait()

    def normed_of(raw):
        raw = raw.astype(jnp.float32)
        mean_sq = jnp.mean(raw * raw, axis=-1, keepdims=True)
        return (raw * lax.rsqrt(mean_sq + 1e-6) * in_gain[...]).astype(jnp.bfloat16)

    for copy in first_copies:
        copy.wait_recv()
    ids = jnp.zeros((8, 1), jnp.int32)
    line = lax.broadcasted_iota(jnp.int32, (8, 1), 0)
    for slot, at in enumerate(slot_chips(chip, chips)):
        ids = jnp.where(line == slot, at * 2 + core, ids)
    for side, query_view in enumerate((me, partner)):
        listed = lists[side]
        valid = lax.broadcasted_iota(jnp.int32, (8, listed.shape[1]), 1) < counts[side:side + 1, :]
        hits = jnp.where(((listed == ids) | (ids == query_view)) & valid, 1.0, 0.0)
        hit = jnp.max(hits, axis=1, keepdims=True)
        for slot in range(SLOTS):
            mask[side, slot] = jnp.broadcast_to(hit[slot:slot + 1], (8, 2 * rows))

    loads[4].wait()
    query_in = jnp.concatenate([normed_of(buf[0]), normed_of(other[...])], axis=0)
    query = jnp.dot(query_in, wq[...], preferred_element_type=jnp.float32).astype(jnp.bfloat16)
    query = query.astype(jnp.float32) * HEAD_DIM ** (-0.5)
    query_t = query.T.astype(jnp.bfloat16)
    zero = jnp.zeros((HEAD_DIM, rows), jnp.bfloat16)
    for unit in range(heads):
        pair, side = unit % (heads // 2), 1 - unit // (heads // 2)
        first, second = (
            query_t[h * HEAD_DIM:(h + 1) * HEAD_DIM, side * rows:(side + 1) * rows] for h in (2 * pair, 2 * pair + 1)
        )
        qpad[unit] = jnp.concatenate(
            [jnp.concatenate([first, zero], axis=1), jnp.concatenate([zero, second], axis=1)], axis=0
        )
    loads[5].wait()
    loads[6].wait()

    queries = 2 * rows
    tiles = rows // 16

    def project(first, second):
        normed = normed_of(jnp.concatenate([first, second], axis=0))
        chunk = width // 2
        for at in range(2):
            columns = slice(at * chunk, (at + 1) * chunk)
            value = jnp.dot(normed, wv[:, columns], preferred_element_type=jnp.float32)
            vtbuf[at * heads // 4:(at + 1) * heads // 4] = value.T.astype(jnp.bfloat16).reshape(heads // 4, 2 * HEAD_DIM, rows)
        for at in range(2):
            key = jnp.dot(
                normed, wk[:, at * chunk:(at + 1) * chunk], preferred_element_type=jnp.float32
            ).astype(jnp.bfloat16)
            for pair in range(heads // 4):
                kbuf[at * heads // 4 + pair] = key[:, pair * 2 * HEAD_DIM:(pair + 1) * 2 * HEAD_DIM]

    def score(unit, at, scores):
        scores[at] = jnp.dot(kbuf[unit % (heads // 2)], qpad[unit], preferred_element_type=jnp.float32)

    def weigh(h, at, scores, weights, keep_ref, on_first, on_second):
        found = scores[at].reshape(2 * tiles, 8, queries)
        first, second = found[:tiles], found[tiles:]
        old = peaks[h]
        new = jnp.maximum(
            jnp.where(on_first, jnp.max(first, axis=0), -INF),
            jnp.where(on_second, jnp.max(second, axis=0), -INF),
        )
        new = jnp.maximum(old, jnp.broadcast_to(jnp.max(new, axis=0, keepdims=True), (8, queries)))
        e_first = jnp.exp(first - jnp.where(on_first, new, INF)[None])
        e_second = jnp.exp(second - jnp.where(on_second, new, INF)[None])
        keep = jnp.exp(old - new)
        peaks[h] = new
        keep_ref[at] = keep
        totals[h] = totals[h] * keep + (jnp.sum(e_first, axis=0) + jnp.sum(e_second, axis=0))
        weights[at] = jnp.concatenate([e_first, e_second], axis=0).reshape(rows, queries).astype(jnp.bfloat16)

    def gather(unit, at, weights, keep_ref):
        kept = acc[unit].reshape(HEAD_DIM // 8, 8, queries) * keep_ref[at][None]
        found = jnp.dot(vtbuf[unit % (heads // 2)], weights[at], preferred_element_type=jnp.float32)
        found = jnp.concatenate([found[:HEAD_DIM, :rows], found[HEAD_DIM:, rows:]], axis=1)
        acc[unit] = kept.reshape(HEAD_DIM, queries) + found

    def attend(near, far, handed=None):
        masks = [(mask[side, near] > 0.5, mask[side, far] > 0.5) for side in range(2)]
        sides = ((s_even, w_even, keeps.at[0]), (s_odd, w_odd, keeps.at[1]))

        def score_all(group, scores):
            for at in range(GROUP):
                score(GROUP * group + at, at, scores)

        def gather_all(group, weights, keep):
            for at in range(GROUP):
                gather(GROUP * group + at, at, weights, keep)

        def stage(group, odd, ahead=True, behind=True):
            scores, weights, keep = sides[odd]
            next_scores, last_weights, last_keep = sides[1 - odd]
            if ahead:
                score_all(group + 1, next_scores)
            if behind:
                gather_all(group - 1, last_weights, last_keep)
            for at in range(GROUP):
                weigh(GROUP * group + at, at, scores, weights, keep, *masks[1 - 2 * group // groups])

        score_all(0, s_even)
        stage(0, 0, behind=False)
        if handed is None:
            for group in range(1, groups - 1):
                stage(group, group % 2)
        else:
            for group in range(1, groups - 1):
                stage(group, group % 2)
                if group <= groups // 2:
                    handed(group - 1)
        stage(groups - 1, 1, ahead=False)
        gather_all(groups - 1, w_odd, keeps.at[1])

    def pick(table, j):
        found = table[0]
        for at in range(1, len(table)):
            found = jnp.where(j == at, table[at], found)
        return found

    def step(j, carry):
        if grid:
            picks = [
                jnp.where(outer, pick(far, j), pick(near, j))
                for far, near in zip(zip(*OUTER_STEPS), zip(*INNER_STEPS))
            ]
        else:
            picks = [pick(column, j) for column in zip(*OUTER_STEPS)]
        near, near_half, far, far_half = picks
        near_row = pl.multiple_of(near_half * half, half)
        far_row = pl.multiple_of(far_half * half, half)
        project(buf[near, pl.ds(near_row, half)], buf[far, pl.ds(far_row, half)])
        poll(j, 0)
        attend(near, far)
        poll(j, 1)
        return carry

    lax.fori_loop(0, steps, step, 0)

    def stats_swap(group):
        return partner_copy(stats_out.at[group], stats_in.at[group], 3 + group)

    def acc_swap(group):
        members = pl.ds(group * GROUP, GROUP)
        return partner_copy(acc.at[members], acc_in.at[members], 3 + groups // 2 + group)

    def total_of(unit):
        return jnp.sum(totals[unit], axis=0, keepdims=True)

    def hand(group):
        acc_swap(group).start()
        members = range(group * GROUP, (group + 1) * GROUP)
        stats_out[group] = jnp.concatenate(
            [peaks[unit][:1] for unit in members] + [total_of(unit) for unit in members], axis=0
        )
        stats_swap(group).start()

    if grid:
        near, far = (jnp.where(outer, OUTER_STEPS[-1][at], INNER_STEPS[-1][at]) for at in (0, 2))
    else:
        near, far = (jnp.int32(OUTER_STEPS[-1][at]) for at in (0, 2))
    span = pl.ds(half, half)
    project(buf[near, span], buf[far, span])
    attend(near, far, hand)

    for part in range(PARTS):
        for kind in range(6):
            send(kind, None, 1, part, partner).wait_send()
        if grid:
            @pl.when(jnp.logical_not(outer))
            def _(part=part):
                send(6, None, 1, part, partner).wait_send()
    for copy in first_copies:
        copy.wait_send()
    loads[7].wait()
    loads[8].wait()
    update = buf[0].astype(jnp.float32)
    for group in range(groups // 2):
        stats_swap(group).wait_recv()
        acc_swap(group).wait_recv()
        for duo in range(2):
            pieces = []
            for at in (2 * duo, 2 * duo + 1):
                theirs = group * GROUP + at
                mine = heads // 2 + theirs
                peak, peak_in = peaks[mine][:1], stats_in[group, at:at + 1, :]
                new = jnp.maximum(peak, peak_in)
                keep, keep_in = jnp.exp(peak - new), jnp.exp(peak_in - new)
                total = total_of(mine) * keep + stats_in[group, GROUP + at:GROUP + at + 1, :] * keep_in
                attended = (acc[mine] * keep + acc_in[theirs] * keep_in) / total
                mean_sq = jnp.mean(attended * attended, axis=0, keepdims=True)
                found = attended * lax.rsqrt(mean_sq + 1e-6)
                pieces += [found[:, :rows], found[:, rows:]]
            start = (group * GROUP + 2 * duo) * 2 * HEAD_DIM
            feats = slice(start, start + 4 * HEAD_DIM)
            head_normed = (jnp.concatenate(pieces, axis=0).T * out_gain[:, feats]).astype(jnp.bfloat16)
            update = update + jnp.dot(head_normed, wo[feats, :], preferred_element_type=jnp.float32)
    out_ref[...] = update.astype(out_ref.dtype)

    for group in range(groups // 2):
        stats_swap(group).wait_send()
        acc_swap(group).wait_send()


def on_device(tokens, in_gain, w_query, w_key, w_value, w_out, out_gain, covis_list, covis_count):
    views = lax.axis_size("views")
    rows, width = tokens.shape[1:]
    slots_listed = covis_list.shape[1]
    hbm = pl.BlockSpec(memory_space=pltpu.HBM)
    vmem = pl.BlockSpec(memory_space=pltpu.VMEM)
    bf16, f32 = jnp.bfloat16, jnp.float32
    heads = width // HEAD_DIM
    dma = pltpu.SemaphoreType.DMA
    out = pl.pallas_call(
        functools.partial(body, views),
        out_shape=jax.ShapeDtypeStruct((rows, width), tokens.dtype),
        in_specs=[hbm] * 9,
        out_specs=vmem,
        scratch_shapes=[
            pltpu.VMEM((SLOTS, rows, width), bf16),
            pltpu.VMEM((rows, width), bf16),
            pltpu.VMEM((width, width), bf16),
            pltpu.VMEM((width, width), bf16),
            pltpu.VMEM((width, width), bf16),
            pltpu.VMEM((width, width), bf16),
            pltpu.VMEM((1, width), f32),
            pltpu.VMEM((1, width), f32),
            pltpu.VMEM((2, 1, slots_listed), jnp.int32),
            pltpu.VMEM((2, 1), jnp.int32),
            pltpu.VMEM((heads, 2 * HEAD_DIM, 2 * rows), bf16),
            pltpu.VMEM((heads // 2, rows, 2 * HEAD_DIM), bf16),
            pltpu.VMEM((heads // 2, 2 * HEAD_DIM, rows), bf16),
            pltpu.VMEM((heads, 8, 2 * rows), f32),
            pltpu.VMEM((heads, 8, 2 * rows), f32),
            pltpu.VMEM((heads, HEAD_DIM, 2 * rows), f32),
            pltpu.VMEM((2, SLOTS, 8, 2 * rows), f32),
            pltpu.VMEM((heads // GROUP // 2, 2 * GROUP, 2 * rows), f32),
            pltpu.VMEM((heads // GROUP // 2, 2 * GROUP, 2 * rows), f32),
            pltpu.VMEM((heads // 2, HEAD_DIM, 2 * rows), f32),
            pltpu.VMEM((GROUP, rows, 2 * rows), f32),
            pltpu.VMEM((GROUP, rows, 2 * rows), f32),
            pltpu.VMEM((GROUP, rows, 2 * rows), bf16),
            pltpu.VMEM((GROUP, rows, 2 * rows), bf16),
            pltpu.VMEM((2, GROUP, 8, 2 * rows), f32),
            dma((9,)),
            dma((8, PARTS)),
            dma((SLOTS, PARTS)),
            dma((3 + heads // GROUP,)),
            dma((3 + heads // GROUP,)),
        ],
        compiler_params=pltpu.CompilerParams(
            collective_id=0, has_side_effects=True, vmem_limit_bytes=32 * 1024 * 1024
        ),
    )(*(pltpu.with_memory_space_constraint(a, pltpu.HBM) for a in (tokens[0], in_gain[None], w_query, w_key, w_value, w_out, out_gain[None], covis_list)), covis_count)
    return out[None]


def solution(mesh):
    in_specs = (
        P(("groups", "views"), None, None),
        P(), P(), P(), P(), P(), P(),
        P(("groups", "views"), None),
        P(("groups", "views")),
    )
    out_specs = P(("groups", "views"), None, None)
    return jax.shard_map(on_device, mesh=mesh, in_specs=in_specs, out_specs=out_specs, check_vma=False)
```

```python
import functools

import jax
import jax.numpy as jnp
from jax import lax
from jax.experimental import pallas as pl
from jax.experimental.pallas import tpu as pltpu
from jax.sharding import PartitionSpec as P

HEADS = 16
HEAD_DIM = 64
REACH = 6
SPAN = REACH // 2
SLOTS = 2 * SPAN + 2
RELAY = SLOTS - 1
PARTS = 4
ROUNDS = SPAN * PARTS
GROUP = 4
MESH = pl.DeviceIdType.MESH
INF = float("inf")
LOW = -3e38


def is_grid(chips):
    return chips == 2 * SPAN + 2


def grid_chip(chip, mirror, depth, side):
    z, y = chip // 2, chip % 2
    if depth:
        z = z + 1 - 2 * (z % 2)
    if mirror:
        z = 3 - z
    if side:
        y = 1 - y
    return 2 * z + y


OUTER_SLOTS = ((0, 0, 0), (0, 1, 0), (0, 0, 1), (1, 0, 0), (0, 1, 1), (1, 1, 1), (1, 0, 1))
INNER_SLOTS = ((0, 0, 0), (0, 1, 0), (0, 0, 1), (0, 1, 1), (1, 1, 1), (1, 0, 1), (1, 0, 0))
INNER_STEPS = ((0, 0, 0, 1), (2, 0, 2, 1), (1, 0, 4, 0), (1, 1, 4, 1), (5, 0, 5, 1), (3, 0, 6, 0), (3, 1, 6, 1))
OUTER_STEPS = ((0, 0, 0, 1),) + tuple(
    (1 + 2 * group, late, 2 + 2 * group, late) for group in range(SPAN) for late in range(2)
)


def slot_chips(chip, chips):
    if is_grid(chips):
        outer = (chip // 2) % 3 == 0
        return [
            jnp.where(outer, grid_chip(chip, *far), grid_chip(chip, *near))
            for far, near in zip(OUTER_SLOTS, INNER_SLOTS)
        ]
    found = [chip]
    for hops in range(1, SPAN + 1):
        found += [(chip - hops + chips) % chips, (chip + hops) % chips]
    return found


def body(
    views, tok_hbm, in_gain_hbm, wq_hbm, wk_hbm, wv_hbm, wo_hbm, out_gain_hbm, list_hbm, count_hbm,
    out_ref,
    buf, other, wq, wk, wv, wo, in_gain, out_gain, lists, counts, qpad, kbuf, vtbuf,
    peaks, totals, acc, mask, stats_out, stats_in, acc_in,
    s_even, s_odd, w_even, w_odd, keeps,
    load_sem, send_sem, recv_sem, misc_send, misc_recv,
):
    chips = views // 2
    grid = is_grid(chips)
    me = lax.axis_index("views")
    chip, core = me // 2, me % 2
    partner = chip * 2 + 1 - core
    rows, width = tok_hbm.shape
    heads = width // HEAD_DIM
    size = rows // PARTS
    half = rows // 2
    steps = ROUNDS // 2
    groups = heads // GROUP

    loads = [
        pltpu.make_async_copy(tok_hbm, buf.at[0], load_sem.at[0]),
        pltpu.make_async_copy(in_gain_hbm, in_gain, load_sem.at[5]),
        pltpu.make_async_copy(list_hbm, lists.at[0], load_sem.at[7]),
        pltpu.make_async_copy(count_hbm, counts.at[0], load_sem.at[8]),
        pltpu.make_async_copy(wq_hbm, wq, load_sem.at[1]),
        pltpu.make_async_copy(wk_hbm, wk, load_sem.at[2]),
        pltpu.make_async_copy(wv_hbm, wv, load_sem.at[3]),
        pltpu.make_async_copy(out_gain_hbm, out_gain, load_sem.at[6]),
        pltpu.make_async_copy(wo_hbm, wo, load_sem.at[4]),
    ]

    if grid:
        outer = (chip // 2) % 3 == 0
        beside = grid_chip(chip, 0, 0, 1) * 2 + core
        along = grid_chip(chip, 0, 1, 0) * 2 + core
        across = grid_chip(chip, 1, 0, 0) * 2 + core
        skip = grid_chip(chip, 1, 1, 0) * 2 + core
    else:
        outer = None
        beside = (chip + chips - 1) % chips * 2 + core
        along = (chip + 1) % chips * 2 + core

    barrier = pltpu.get_barrier_semaphore()
    for device in (partner, beside, along):
        pl.semaphore_signal(barrier, inc=1, device_id={"views": device}, device_id_type=MESH)
    if grid:
        @pl.when(jnp.logical_not(outer))
        def _():
            for device in (across, skip):
                pl.semaphore_signal(barrier, inc=1, device_id={"views": device}, device_id_type=MESH)
    for load in loads:
        load.start()
    pl.semaphore_wait(barrier, 4 if grid else 3)

    def send(kind, source, slot, part, device):
        span = pl.ds(pl.multiple_of(part * size, size), size)
        return pltpu.make_async_remote_copy(
            src_ref=tok_hbm.at[span] if source is None else buf.at[source, span],
            dst_ref=buf.at[slot, span],
            send_sem=send_sem.at[kind, part],
            recv_sem=recv_sem.at[slot, part],
            device_id={"views": device},
            device_id_type=MESH,
        )

    def arrived(slot, part):
        send(0, slot, slot, part, partner).wait_recv()

    def partner_copy(src, dst, index):
        return pltpu.make_async_remote_copy(
            src_ref=src, dst_ref=dst, send_sem=misc_send.at[index], recv_sem=misc_recv.at[index],
            device_id={"views": partner}, device_id_type=MESH,
        )

    first_copies = [
        partner_copy(tok_hbm, other, 0),
        partner_copy(list_hbm, lists.at[1], 1),
        partner_copy(count_hbm, counts.at[1], 2),
    ]
    if grid:
        @pl.when(outer)
        def _():
            for part in range(PARTS):
                send(2, None, 2, part, beside).start()
                send(0, None, RELAY, part, skip).start()
            for part in range(PARTS):
                send(1, None, 1, part, along).start()

        @pl.when(jnp.logical_not(outer))
        def _():
            for part in range(PARTS):
                send(0, None, 1, part, along).start()
                send(1, None, 2, part, beside).start()
    else:
        for part in range(PARTS):
            send(0, None, 1, part, along).start()
            send(1, None, 2, part, beside).start()
    for copy in first_copies:
        copy.start()

    def ring_poll(r):
        group, part = r // PARTS, r % PARTS
        arrived(1 + 2 * group, part)
        arrived(2 + 2 * group, part)

        @pl.when(group < SPAN - 1)
        def _():
            send(2 + 2 * group, 1 + 2 * group, 3 + 2 * group, part, along).start()
            send(3 + 2 * group, 2 + 2 * group, 4 + 2 * group, part, beside).start()

    def outer_poll(r):
        group, part = r // PARTS, r % PARTS
        arrived(1 + 2 * group, part)

        @pl.when(group < 2)
        def _():
            send(3 + group, 1 + 2 * group, 4 + 2 * group, part, beside).start()
        arrived(2 + 2 * group, part)

        @pl.when(group == 0)
        def _():
            send(5, 2, 3, part, along).start()

    def far_on(part):
        arrived(RELAY, part)
        send(3, RELAY, 3, part, along).start()
        send(4, RELAY, 4, part, beside).start()

    def corner_on(part):
        arrived(5, part)
        send(5, 5, 5, part, along).start()

    def inner_poll(r):
        if 1 <= r < 5:
            far_on(r - 1)
        if r < PARTS:
            arrived(2, r)
        if r == 2:
            for part in range(3):
                send(6, 2, 5, part, across).start()
        if r == 3:
            send(6, 2, 5, 3, across).start()
            for part in range(PARTS):
                send(2, None, 6, part, across).start()
        if 5 <= r < 9:
            corner_on(r - 5)
        if 4 <= r < 8:
            arrived(1, r - 4)
            arrived(4, r - 4)
        if 8 <= r < 12:
            arrived(3, r - 8)
        if 9 <= r:
            arrived(6, r - 9)

    inner_polls = {
        0: ((0,), (1, 2, 3)), 1: ((4,), (5,)), 2: ((6,), (7,)), 3: ((), (8,)), 4: ((9,), (10,)), 5: ((11,), (12,)),
    }

    def poll(j, second):
        ahead = j < steps
        if not grid:
            @pl.when(ahead)
            def _():
                ring_poll(2 * j + second)
            return

        @pl.when(jnp.logical_and(outer, ahead))
        def _():
            outer_poll(2 * j + second)

        @pl.when(jnp.logical_not(outer))
        def _():
            for at, polls in inner_polls.items():
                if polls[second]:
                    @pl.when(j == at)
                    def _(polls=polls):
                        for r in polls[second]:
                            inner_poll(r)

    peaks[...] = jnp.full(peaks.shape, LOW, jnp.float32)
    totals[...] = jnp.zeros(totals.shape, jnp.float32)
    acc[...] = jnp.zeros(acc.shape, jnp.float32)
    for load in loads[:4]:
        load.wait()

    def normed_of(raw):
        raw = raw.astype(jnp.float32)
        mean_sq = jnp.mean(raw * raw, axis=-1, keepdims=True)
        return (raw * lax.rsqrt(mean_sq + 1e-6) * in_gain[...]).astype(jnp.bfloat16)

    for copy in first_copies:
        copy.wait_recv()
    ids = jnp.zeros((8, 1), jnp.int32)
    line = lax.broadcasted_iota(jnp.int32, (8, 1), 0)
    for slot, at in enumerate(slot_chips(chip, chips)):
        ids = jnp.where(line == slot, at * 2 + core, ids)
    for side, query_view in enumerate((me, partner)):
        listed = lists[side]
        valid = lax.broadcasted_iota(jnp.int32, (8, listed.shape[1]), 1) < counts[side:side + 1, :]
        hits = jnp.where(((listed == ids) | (ids == query_view)) & valid, 1.0, 0.0)
        hit = jnp.max(hits, axis=1, keepdims=True)
        for slot in range(SLOTS):
            mask[side, slot] = jnp.broadcast_to(hit[slot:slot + 1], (8, 2 * rows))

    loads[4].wait()
    query_in = jnp.concatenate([normed_of(buf[0]), normed_of(other[...])], axis=0)
    query = jnp.dot(query_in, wq[...], preferred_element_type=jnp.float32).astype(jnp.bfloat16)
    query = query.astype(jnp.float32) * HEAD_DIM ** (-0.5)
    query_t = query.T.astype(jnp.bfloat16)
    zero = jnp.zeros((HEAD_DIM, rows), jnp.bfloat16)
    for unit in range(heads):
        pair, side = unit % (heads // 2), 1 - unit // (heads // 2)
        first, second = (
            query_t[h * HEAD_DIM:(h + 1) * HEAD_DIM, side * rows:(side + 1) * rows] for h in (2 * pair, 2 * pair + 1)
        )
        qpad[unit] = jnp.concatenate(
            [jnp.concatenate([first, zero], axis=1), jnp.concatenate([zero, second], axis=1)], axis=0
        )
    loads[5].wait()
    loads[6].wait()

    queries = 2 * rows
    tiles = rows // 16

    def project(first, second):
        normed = normed_of(jnp.concatenate([first, second], axis=0))
        chunk = width // 2
        for at in range(2):
            columns = slice(at * chunk, (at + 1) * chunk)
            value = jnp.dot(normed, wv[:, columns], preferred_element_type=jnp.float32)
            vtbuf[at * heads // 4:(at + 1) * heads // 4] = value.T.astype(jnp.bfloat16).reshape(heads // 4, 2 * HEAD_DIM, rows)
        for at in range(2):
            key = jnp.dot(
                normed, wk[:, at * chunk:(at + 1) * chunk], preferred_element_type=jnp.float32
            ).astype(jnp.bfloat16)
            for pair in range(heads // 4):
                kbuf[at * heads // 4 + pair] = key[:, pair * 2 * HEAD_DIM:(pair + 1) * 2 * HEAD_DIM]

    def score(unit, at, scores):
        scores[at] = jnp.dot(kbuf[unit % (heads // 2)], qpad[unit], preferred_element_type=jnp.float32)

    def weigh(h, at, scores, weights, keep_ref, on_first, on_second):
        found = scores[at].reshape(2 * tiles, 8, queries)
        first, second = found[:tiles], found[tiles:]
        old = peaks[h]
        new = jnp.maximum(
            jnp.where(on_first, jnp.max(first, axis=0), -INF),
            jnp.where(on_second, jnp.max(second, axis=0), -INF),
        )
        new = jnp.maximum(old, jnp.broadcast_to(jnp.max(new, axis=0, keepdims=True), (8, queries)))
        e_first = jnp.exp(first - jnp.where(on_first, new, INF)[None])
        e_second = jnp.exp(second - jnp.where(on_second, new, INF)[None])
        keep = jnp.exp(old - new)
        peaks[h] = new
        keep_ref[at] = keep
        totals[h] = totals[h] * keep + (jnp.sum(e_first, axis=0) + jnp.sum(e_second, axis=0))
        weights[at] = jnp.concatenate([e_first, e_second], axis=0).reshape(rows, queries).astype(jnp.bfloat16)

    def gather(unit, at, weights, keep_ref):
        kept = acc[unit].reshape(HEAD_DIM // 8, 8, queries) * keep_ref[at][None]
        found = jnp.dot(vtbuf[unit % (heads // 2)], weights[at], preferred_element_type=jnp.float32)
        found = jnp.concatenate([found[:HEAD_DIM, :rows], found[HEAD_DIM:, rows:]], axis=1)
        acc[unit] = kept.reshape(HEAD_DIM, queries) + found

    def attend(near, far, handed=None):
        masks = [(mask[side, near] > 0.5, mask[side, far] > 0.5) for side in range(2)]
        sides = ((s_even, w_even, keeps.at[0]), (s_odd, w_odd, keeps.at[1]))

        def score_all(group, scores):
            for at in range(GROUP):
                score(GROUP * group + at, at, scores)

        def gather_all(group, weights, keep):
            for at in range(GROUP):
                gather(GROUP * group + at, at, weights, keep)

        def stage(group, odd, ahead=True, behind=True):
            scores, weights, keep = sides[odd]
            next_scores, last_weights, last_keep = sides[1 - odd]
            if ahead:
                score_all(group + 1, next_scores)
            if behind:
                gather_all(group - 1, last_weights, last_keep)
            for at in range(GROUP):
                weigh(GROUP * group + at, at, scores, weights, keep, *masks[1 - 2 * group // groups])

        score_all(0, s_even)
        stage(0, 0, behind=False)
        if handed is None:
            for group in range(1, groups - 1):
                stage(group, group % 2)
        else:
            for group in range(1, groups - 1):
                stage(group, group % 2)
                if group <= groups // 2:
                    handed(group - 1)
        stage(groups - 1, 1, ahead=False)
        gather_all(groups - 1, w_odd, keeps.at[1])

    def pick(table, j):
        found = table[0]
        for at in range(1, len(table)):
            found = jnp.where(j == at, table[at], found)
        return found

    def step(j, carry):
        if grid:
            picks = [
                jnp.where(outer, pick(far, j), pick(near, j))
                for far, near in zip(zip(*OUTER_STEPS), zip(*INNER_STEPS))
            ]
        else:
            picks = [pick(column, j) for column in zip(*OUTER_STEPS)]
        near, near_half, far, far_half = picks
        near_row = pl.multiple_of(near_half * half, half)
        far_row = pl.multiple_of(far_half * half, half)
        project(buf[near, pl.ds(near_row, half)], buf[far, pl.ds(far_row, half)])
        poll(j, 0)
        attend(near, far)
        poll(j, 1)
        return carry

    lax.fori_loop(0, steps, step, 0)

    def stats_swap(group):
        return partner_copy(stats_out.at[group], stats_in.at[group], 3 + group)

    def acc_swap(group):
        members = pl.ds(group * GROUP, GROUP)
        return partner_copy(acc.at[members], acc_in.at[members], 3 + groups // 2 + group)

    def total_of(unit):
        return jnp.sum(totals[unit], axis=0, keepdims=True)

    def hand(group):
        acc_swap(group).start()
        members = range(group * GROUP, (group + 1) * GROUP)
        stats_out[group] = jnp.concatenate(
            [peaks[unit][:1] for unit in members] + [total_of(unit) for unit in members], axis=0
        )
        stats_swap(group).start()

    if grid:
        near, far = (jnp.where(outer, OUTER_STEPS[-1][at], INNER_STEPS[-1][at]) for at in (0, 2))
    else:
        near, far = (jnp.int32(OUTER_STEPS[-1][at]) for at in (0, 2))
    span = pl.ds(half, half)
    project(buf[near, span], buf[far, span])
    attend(near, far, hand)

    for part in range(PARTS):
        for kind in range(6):
            send(kind, None, 1, part, partner).wait_send()
        if grid:
            @pl.when(jnp.logical_not(outer))
            def _(part=part):
                send(6, None, 1, part, partner).wait_send()
    for copy in first_copies:
        copy.wait_send()
    loads[7].wait()
    loads[8].wait()
    update = buf[0].astype(jnp.float32)
    for group in range(groups // 2):
        stats_swap(group).wait_recv()
        acc_swap(group).wait_recv()
        for duo in range(2):
            pieces = []
            for at in (2 * duo, 2 * duo + 1):
                theirs = group * GROUP + at
                mine = heads // 2 + theirs
                peak, peak_in = peaks[mine][:1], stats_in[group, at:at + 1, :]
                new = jnp.maximum(peak, peak_in)
                keep, keep_in = jnp.exp(peak - new), jnp.exp(peak_in - new)
                total = total_of(mine) * keep + stats_in[group, GROUP + at:GROUP + at + 1, :] * keep_in
                attended = (acc[mine] * keep + acc_in[theirs] * keep_in) / total
                mean_sq = jnp.mean(attended * attended, axis=0, keepdims=True)
                found = attended * lax.rsqrt(mean_sq + 1e-6)
                pieces += [found[:, :rows], found[:, rows:]]
            start = (group * GROUP + 2 * duo) * 2 * HEAD_DIM
            feats = slice(start, start + 4 * HEAD_DIM)
            head_normed = (jnp.concatenate(pieces, axis=0).T * out_gain[:, feats]).astype(jnp.bfloat16)
            update = update + jnp.dot(head_normed, wo[feats, :], preferred_element_type=jnp.float32)
    out_ref[...] = update.astype(out_ref.dtype)

    for group in range(groups // 2):
        stats_swap(group).wait_send()
        acc_swap(group).wait_send()


def on_device(tokens, in_gain, w_query, w_key, w_value, w_out, out_gain, covis_list, covis_count):
    views = lax.axis_size("views")
    rows, width = tokens.shape[1:]
    slots_listed = covis_list.shape[1]
    hbm = pl.BlockSpec(memory_space=pltpu.HBM)
    vmem = pl.BlockSpec(memory_space=pltpu.VMEM)
    bf16, f32 = jnp.bfloat16, jnp.float32
    heads = width // HEAD_DIM
    dma = pltpu.SemaphoreType.DMA
    out = pl.pallas_call(
        functools.partial(body, views),
        out_shape=jax.ShapeDtypeStruct((rows, width), tokens.dtype),
        in_specs=[hbm] * 9,
        out_specs=vmem,
        scratch_shapes=[
            pltpu.VMEM((SLOTS, rows, width), bf16),
            pltpu.VMEM((rows, width), bf16),
            pltpu.VMEM((width, width), bf16),
            pltpu.VMEM((width, width), bf16),
            pltpu.VMEM((width, width), bf16),
            pltpu.VMEM((width, width), bf16),
            pltpu.VMEM((1, width), f32),
            pltpu.VMEM((1, width), f32),
            pltpu.VMEM((2, 1, slots_listed), jnp.int32),
            pltpu.VMEM((2, 1), jnp.int32),
            pltpu.VMEM((heads, 2 * HEAD_DIM, 2 * rows), bf16),
            pltpu.VMEM((heads // 2, rows, 2 * HEAD_DIM), bf16),
            pltpu.VMEM((heads // 2, 2 * HEAD_DIM, rows), bf16),
            pltpu.VMEM((heads, 8, 2 * rows), f32),
            pltpu.VMEM((heads, 8, 2 * rows), f32),
            pltpu.VMEM((heads, HEAD_DIM, 2 * rows), f32),
            pltpu.VMEM((2, SLOTS, 8, 2 * rows), f32),
            pltpu.VMEM((heads // GROUP // 2, 2 * GROUP, 2 * rows), f32),
            pltpu.VMEM((heads // GROUP // 2, 2 * GROUP, 2 * rows), f32),
            pltpu.VMEM((heads // 2, HEAD_DIM, 2 * rows), f32),
            pltpu.VMEM((GROUP, rows, 2 * rows), f32),
            pltpu.VMEM((GROUP, rows, 2 * rows), f32),
            pltpu.VMEM((GROUP, rows, 2 * rows), bf16),
            pltpu.VMEM((GROUP, rows, 2 * rows), bf16),
            pltpu.VMEM((2, GROUP, 8, 2 * rows), f32),
            dma((9,)),
            dma((8, PARTS)),
            dma((SLOTS, PARTS)),
            dma((3 + heads // GROUP,)),
            dma((3 + heads // GROUP,)),
        ],
        compiler_params=pltpu.CompilerParams(
            collective_id=0, has_side_effects=True, vmem_limit_bytes=32 * 1024 * 1024
        ),
    )(*(pltpu.with_memory_space_constraint(a, pltpu.HBM) for a in (tokens[0], in_gain[None], w_query, w_key, w_value, w_out, out_gain[None], covis_list)), covis_count)
    return out[None]


def solution(mesh):
    in_specs = (
        P(("groups", "views"), None, None),
        P(), P(), P(), P(), P(), P(),
        P(("groups", "views"), None),
        P(("groups", "views")),
    )
    out_specs = P(("groups", "views"), None, None)
    return jax.shard_map(on_device, mesh=mesh, in_specs=in_specs, out_specs=out_specs, check_vma=False)
```
